256 devices in a mesh: region: 64 (over x, z, core), level: 4 (over y).
Axes of the slice: x: 4, y: 4, z: 8, core: 2. Of those that a mesh axis runs over, the one named last changes fastest.
Arguments:
- ensemble: bfloat16 [4, 256, 262144], P('level', None, 'region'), may hold values from -6 to 6
- obs_anomaly: bfloat16 [4, 65536, 256], P('level', 'region'), may hold values from -6 to 6
- innovation: bfloat16 [4, 65536], P('level', 'region'), may hold values from -18 to 18
- obs_precision: bfloat16 [4, 65536], P('level', 'region'), may hold values from 0.019897461 to 0.29882812
- owner_region: int32 [4, 65536, 1], P('level', 'region'), may hold values from 0 to 63; in each aligned block of 1024 rows (0 to 1023, 1024 to 2047, ..., all dimensions but the last counted through in order) at most 24 rows name the same one
- neighbours: int32 [64, 3], replicated, may hold values from 0 to 63, all different within a row
Outputs:
- analysis: bfloat16 [4, 256, 262144], P('level', None, 'region')
The draws below stay inside these ranges and needn't reach their ends.
Inputs may be any that keep to these rules, and one draw needn't show every extreme that they name: `owner_region`: among the 1024 observations of one device (aligned blocks), no region is named more than 24 times, a bound that some block reaches. `neighbours`: each row lists 3 different regions; every region is listed by some row.
All inputs are finite; a program needn't handle non-finite values.
Results may differ from the reference program's by a relative error of at most 0.0059.
Values may be sent and summed in bfloat16 or wider, within the bound.
No kernel may reach another device: no remote copies, remote signals or barrier semaphores. Data moves between devices by JAX's collectives and lax.ppermute only.
A program may use at most 64 MiB of HBM per device.

```python
import math
import jax
import jax.numpy as jnp
import numpy as np
from jax import lax

MEMBERS = 256
NEIGH = 3
NSTEPS = 4
COL_DEV = 4096
OBS_DEV = 1024
REGIONS = 64
LEVELS = 4
CAP = 24
SLOTS = 96
COLS = 262144
OBS = 65536


def draw_obs_anomaly(key, part):
    pattern_key = jax.random.fold_in(key, 11)
    sign_key = jax.random.fold_in(key, 12)
    noise_key = jax.random.fold_in(key, 13)
    pattern = jnp.clip(jax.random.normal(pattern_key, (LEVELS, 1, MEMBERS), jnp.float32), -3.5, 3.5)
    flips = jax.random.bernoulli(sign_key, 0.5, (LEVELS, OBS, 1))
    signs = jnp.where(flips, 1.0, -1.0).astype(jnp.float32)
    noise = jax.random.normal(noise_key, (LEVELS, OBS, MEMBERS), jnp.float32)
    strength = 0.7
    values = strength * signs * pattern + noise
    return jnp.clip(values, -6.0, 6.0).astype(jnp.bfloat16)


def levels(rng, extent, cuts, smallest, top_value):
    def one(dim, blocks):
        draws = jax.random.uniform(jax.random.fold_in(jax.random.fold_in(rng, 6), dim), (blocks,), jnp.float32, smallest / len(cuts), top_value / len(cuts))
        return jnp.repeat(jnp.exp(draws), extent[dim] // blocks).reshape((-1,) + (1,) * (len(extent) - dim - 1))

    loudness = one(*cuts[0])
    for cut in cuts[1:]:
        loudness = loudness * one(*cut)
    return loudness


def picks_of(own_key, rows, count, top, lift):
    ranking = jax.random.permutation(jax.random.fold_in(own_key, 1), count)
    favour = ranking
    for power in range(3):
        favour = favour * favour // count
    favour = favour * lift // count
    tickets = jax.random.randint(jax.random.fold_in(own_key, 2), (rows, count), 0, 4096) + favour
    sure = jax.random.permutation(jax.random.fold_in(own_key, 3), rows)[jnp.arange(count) % rows]
    tickets = jnp.where(jnp.arange(rows)[:, None] == sure[None, :], 1 << 14, tickets)
    merit = tickets * count + jnp.arange(count)
    return lax.top_k(merit.astype(jnp.int32), top)[1].astype(jnp.int32)


def deal_out(stream_key, own, number, rows, count, top, bound, slope):
    sequence = jax.random.permutation(stream_key, count)
    packed, usual = load_shares(count, rows * top, bound, slope, True), load_shares(count, rows * top, bound, slope, False)
    places = jnp.arange(count)

    def named(sizes, rotation):
        used = int((sizes > 0).sum())
        fixed = max(1, used // 4)
        shifted = fixed + (places - fixed + rotation * (used - fixed)) % max(1, count - fixed)
        return jnp.zeros((count,), jnp.int32).at[sequence[jnp.where(places < fixed, places, shifted)]].set(jnp.asarray(sizes, jnp.int32))

    sizes = jnp.where(number % 4 == 0, named(packed, number // 4), named(usual, number - number // 4 - 1))
    mixed = jax.random.permutation(jax.random.fold_in(own, 3), count)
    giver, receiver = mixed[0:count // 2 * 2:2], mixed[1:count // 2 * 2:2]
    slack = jnp.minimum(sizes[giver] - 1, bound - sizes[receiver]) // 2
    slack = jnp.where((giver == sequence[0]) | (receiver == sequence[0]) | (sizes[receiver] == 0), 0, jnp.maximum(slack, 0))
    shifted = jax.random.randint(jax.random.fold_in(own, 4), (count // 2,), 0, 1 << 20) % (slack + 1)
    sizes = sizes.at[giver].add(-shifted).at[receiver].add(shifted)
    items = jnp.searchsorted(jnp.cumsum(sizes), jnp.arange(rows * top), side="right").astype(jnp.int32)
    listing = items.reshape(top, rows).T
    listing = listing[jax.random.permutation(jax.random.fold_in(own, 1), rows)]
    rotation = jax.random.randint(jax.random.fold_in(own, 2), (rows, 1), 0, top)
    return jnp.take_along_axis(listing, (jnp.arange(top)[None, :] + rotation) % top, axis=1)


def load_shares(count, total, most, slope, full):
    portions = [(1 << 20) // math.isqrt(grade ** slope) + 1 for grade in range(1, count + 1)]
    largest = most if full else min(most, max(-(-total // count), total * portions[0] // sum(portions)))
    least = 1 if total - largest >= count - 1 else 0
    counts, surplus = [largest] + [least] * (count - 1), total - largest - least * (count - 1)
    while surplus > 0:
        candidates = [i for i in range(1, count) if counts[i] < largest] or [i for i in range(1, count) if counts[i] < most]
        whole, left = sum([portions[i] for i in candidates]), surplus
        for i in candidates:
            extra = min(most - counts[i], max(1, left * portions[i] // whole), surplus)
            counts[i] = counts[i] + extra
            surplus = surplus - extra
    return np.array(counts)


def centred(stream_key, shape, deviation, reach, cuts=(), kind=jnp.bfloat16):
    entries = jax.random.normal(stream_key, shape, jnp.float32) * deviation
    if len(cuts) > 0:
        entries = levels(stream_key, shape, cuts, -0.22, 0.18) * entries
    return jnp.clip(entries, min=-reach, max=reach).astype(kind)


def setup_inputs(seed: int = 0) -> dict:
    seeds = jax.random.split(jax.random.key(seed), 7)
    ensemble = centred(seeds[0], (LEVELS, MEMBERS, COLS), 1.0, 6.0, ((0, 4), (2, 64)))
    obs_anomaly = draw_obs_anomaly(jax.random.fold_in(seeds[6], 71), 0)
    innovation = centred(seeds[2], (LEVELS, OBS), 3.0, 18.0, ((0, 4), (1, 64)))
    obs_precision = jnp.clip(jnp.exp(math.log(0.29882812) - 2.7092764 * jax.random.uniform(seeds[3], (LEVELS, OBS), jnp.float32) ** levels(seeds[3], (LEVELS, OBS), ((0, 4), (1, 64)), -0.2, 0.2)), 0.019897461, 0.29882812).astype(jnp.bfloat16)
    owner_region_keys = jax.random.split(jax.random.fold_in(seeds[4], 1), LEVELS * OBS // OBS_DEV)
    owner_region_turns = jax.random.permutation(jax.random.fold_in(seeds[4], 3), LEVELS * OBS // OBS_DEV)
    owner_region = jax.vmap(lambda own, number: deal_out(jax.random.fold_in(seeds[4], 2), own, number, OBS_DEV, REGIONS, 1, CAP, 2))(owner_region_keys, owner_region_turns).reshape((LEVELS, OBS, 1))
    neighbours = picks_of(seeds[5], REGIONS, REGIONS, NEIGH, 0)
    return dict(ensemble=ensemble, obs_anomaly=obs_anomaly, innovation=innovation, obs_precision=obs_precision, owner_region=owner_region, neighbours=neighbours)


TAPER = 0.6

def neighbour_weights(neighbours):
    region_ids = jnp.arange(neighbours.shape[0], dtype=jnp.int32)
    weights = (region_ids[:, None] == region_ids[None, :]).astype(jnp.float32)
    for listed in range(neighbours.shape[1]):
        hit = (neighbours[:, listed][:, None] == region_ids[None, :]).astype(jnp.float32)
        weights = weights + TAPER ** (listed + 1) * hit
    return weights

def inverse_root(matrix):
    order_size = matrix.shape[0]
    identity = jnp.eye(order_size, dtype=jnp.float32)
    norm_scale = 0.5 * jnp.sqrt(jnp.sum(matrix * matrix))
    root_iter = matrix / norm_scale
    inverse_iter = identity
    for newton_step in range(NSTEPS):
        correction = 1.5 * identity - 0.5 * jnp.dot(inverse_iter, root_iter, precision=lax.Precision.HIGHEST)
        root_iter = jnp.dot(root_iter, correction, precision=lax.Precision.HIGHEST)
        inverse_iter = jnp.dot(correction, inverse_iter, precision=lax.Precision.HIGHEST)
    return inverse_iter / jnp.sqrt(norm_scale)

def analysis_weights(covariance, innovation_sum):
    order_size = covariance.shape[0]
    identity = jnp.eye(order_size, dtype=jnp.float32)
    precision_matrix = covariance + (order_size - 1.0) * identity
    root = inverse_root(precision_matrix)
    inner = jnp.dot(root, innovation_sum, precision=lax.Precision.HIGHEST)
    mean_shift = jnp.dot(root, inner, precision=lax.Precision.HIGHEST)
    return (math.sqrt(order_size - 1.0) * root + mean_shift[:, None]).astype(jnp.bfloat16)

def update_columns(column_block, transform):
    average = lax.optimization_barrier(jnp.mean(column_block.astype(jnp.float32), axis=0))
    anomaly = (column_block.astype(jnp.float32) - average[None, :]).astype(jnp.bfloat16)
    combined = lax.dot_general(transform, anomaly, (((0,), (0,)), ((), ())), preferred_element_type=jnp.float32)
    return (combined + average[None, :]).astype(jnp.bfloat16)

def reference(ensemble, obs_anomaly, innovation, obs_precision, owner_region, neighbours):
    region_weight = neighbour_weights(neighbours)
    owner_ids = owner_region[:, :, 0]
    most_rows = REGIONS * SLOTS

    def one_region(region):
        weight_row = region_weight[region]
        level_covs = []
        level_sums = []
        for source in range(LEVELS):
            obs_weight = weight_row[owner_ids[source]]
            live = obs_weight > 0
            amount = jnp.sum(live.astype(jnp.int32))
            picked = jnp.nonzero(live, size=most_rows, fill_value=0)[0].astype(jnp.int32)
            valid = jnp.arange(most_rows, dtype=jnp.int32) < amount
            gain = (obs_weight[picked] * obs_precision[source][picked].astype(jnp.float32)).astype(jnp.bfloat16)
            gain = jnp.where(valid, gain, jnp.zeros_like(gain))
            picked_rows = obs_anomaly[source][picked]
            weighted = (gain.astype(jnp.float32)[:, None] * picked_rows.astype(jnp.float32)).astype(jnp.bfloat16)
            level_covs.append(jnp.dot(weighted.T, picked_rows, preferred_element_type=jnp.float32))
            level_sums.append(jnp.dot(innovation[source][picked], weighted, preferred_element_type=jnp.float32))
        results = []
        for target in range(LEVELS):
            covariance = jnp.zeros_like(level_covs[0])
            innovation_sum = jnp.zeros_like(level_sums[0])
            for source in range(LEVELS):
                factor = 0.5 ** abs(target - source)
                covariance = covariance + factor * level_covs[source]
                innovation_sum = innovation_sum + factor * level_sums[source]
            transform = analysis_weights(covariance, innovation_sum)
            column_block = lax.dynamic_slice_in_dim(ensemble[target], (region * COL_DEV).astype(jnp.int32), COL_DEV, 1)
            results.append(update_columns(column_block, transform))
        return jnp.stack(results)
    stacked = lax.map(one_region, jnp.arange(REGIONS, dtype=jnp.int32))
    members = ensemble.shape[1]
    return jnp.transpose(stacked, (1, 2, 0, 3)).reshape(LEVELS, members, REGIONS * COL_DEV)
```

```python
import functools
import math

import jax
import jax.numpy as jnp
from jax import lax
from jax.experimental import pallas as pl
from jax.experimental.pallas import tpu as pltpu
from jax.sharding import PartitionSpec as P

NSTEPS = 4
TAPER = 0.6
DECAY = 0.5
LANES = 128
BF16 = jnp.bfloat16
F32 = jnp.float32


def iota(shape, dim):
    return lax.broadcasted_iota(jnp.int32, shape, dim)


def dot(left, right, dims=((1,), (0,))):
    return lax.dot_general(left, right, (dims, ((), ())), preferred_element_type=F32)


def split(value):
    high = value.astype(BF16)
    return high, (value - high.astype(F32)).astype(BF16)


def dot3(left, right):
    lh, ll = left
    rh, rl = right
    return dot(lh, rh) + (dot(lh, rl) + dot(ll, rh))


def place_kernel(regions, capacity, owner_ref, precision_ref, obs_ref, rows_ref):
    count = owner_ref.shape[1]
    blocks = count // LANES
    region_ids = iota((regions, LANES), 0)
    earlier = (iota((LANES, LANES), 0) < iota((LANES, LANES), 1)).astype(BF16)
    counter = jnp.concatenate([earlier, jnp.ones((LANES, LANES), BF16)], axis=1)
    owners = owner_ref[...]
    named = [region_ids == owners[:, b * LANES : (b + 1) * LANES] for b in range(blocks)]
    table = jnp.concatenate([hit.astype(F32).astype(BF16) for hit in named], axis=0)
    ranks = dot(table, counter)
    base = (region_ids * capacity).astype(F32)
    pieces = []
    for b in range(blocks):
        part = ranks[b * regions : (b + 1) * regions]
        slot = jnp.where(named[b], part[:, :LANES] + base, 0.0)
        pieces.append(jnp.sum(slot, axis=0, keepdims=True))
        base = base + part[:, LANES:]
    slots = jnp.concatenate(pieces, axis=1).astype(jnp.int32)
    scale = jnp.sqrt(precision_ref[...].astype(F32))
    obs = obs_ref[...]
    step = 256
    for start in range(0, regions * capacity, step):
        hit = slots == iota((step, count), 0) + start
        placed = jnp.where(hit, scale, 0.0).astype(BF16)
        rows_ref[start : start + step, :] = dot(placed, obs).astype(BF16)


def innovation_kernel(owner_ref, precision_ref, innovation_ref, obs_ref, sums_ref):
    count = owner_ref.shape[1]
    factor = precision_ref[...].astype(F32) * innovation_ref[...].astype(F32)
    table = jnp.where(iota((LANES, count), 0) == owner_ref[...], factor, 0.0).astype(BF16)
    sums_ref[...] = dot(obs_ref[...], table, ((0,), (1,)))


def weight_kernel(regions, levels, neigh, neighbours_ref, high_ref, low_ref, wide_ref):
    size = 2 * regions * levels
    per = 2 * levels
    table = neighbours_ref[...]
    lanes = iota((regions, LANES), 1)
    weight = (iota((regions, LANES), 0) == lanes).astype(F32)
    for listed in range(neigh):
        weight = weight + TAPER ** (listed + 1) * (table[:, listed : listed + 1] == lanes).astype(F32)
    wide = jnp.broadcast_to(weight[:, None, :], (regions, per, LANES)).reshape(size, LANES)
    wide_ref[...] = wide
    high, low = split(wide[:, :regions])
    spread = (iota((regions, size), 1) // per == iota((regions, size), 0)).astype(F32).astype(BF16)
    full = dot(high, spread) + dot(low, spread)
    row = iota((size, size), 0) % per
    col = iota((size, size), 1) % per
    apart = jnp.abs(row // 2 - col // 2)
    factor = jnp.zeros((size, size), F32)
    for distance in range(levels):
        factor = jnp.where(apart == distance, DECAY**distance, factor)
    full = full * jnp.where(row % 2 == col % 2, factor, 0.0)
    high, low = split(full)
    high_ref[...] = high
    low_ref[...] = low


def covariance_kernel(rows_ref, sums_ref, message_ref, scratch_ref):
    half = LANES
    rows = rows_ref[...]
    total = dot(rows, rows, ((0,), (0,)))
    above = iota((half, half), 0) <= iota((half, half), 1)
    same = iota((half, half), 0) == iota((half, half), 1)
    corner = total[half:, half:]
    packed = jnp.concatenate([jnp.where(above, total[:half, :half], corner), total[:half, half:]], axis=0)
    diagonal = jnp.sum(jnp.where(same, corner, 0.0), axis=1, keepdims=True)
    diagonal = jnp.concatenate([diagonal, jnp.zeros_like(diagonal)], axis=0)
    extra = jnp.where(iota((2 * half, LANES), 1) == LANES // 2, diagonal, sums_ref[...])
    scratch_ref[pl.ds(0, 2 * half, 2), :] = packed
    scratch_ref[pl.ds(1, 2 * half, 2), :] = extra
    message_ref[...] = scratch_ref[...].astype(BF16)


def mix_kernel(levels, message_ref, high_ref, low_ref, wide_ref, mixed_ref):
    size = message_ref.shape[0]
    per = 2 * levels
    message = message_ref[...]
    mixed = dot(high_ref[...], message) + dot(low_ref[...], message)
    row = iota((per, size), 0)
    col = iota((per, size), 1)
    apart = jnp.abs(row // 2 - (col % per) // 2)
    factor = jnp.zeros((per, size), F32)
    for distance in range(levels):
        factor = jnp.where(apart == distance, DECAY**distance, factor)
    factor = jnp.where((row % 2 == 1) & (col % 2 == 1), factor, 0.0)
    level_sums = dot(factor.astype(BF16), message)
    level_sums = jnp.where(iota((per, LANES), 1) < LANES // 2, level_sums, 0.0)
    spread = jnp.broadcast_to(level_sums[None], (size // per, per, LANES)).reshape(size, LANES)
    sums = jnp.sum(wide_ref[...] * spread, axis=1, keepdims=True)
    high = sums.astype(BF16).astype(F32)
    odd = iota((size, LANES), 0) % 2 == 1
    lane = iota((size, LANES), 1)
    mixed = jnp.where(odd & (lane == 0), high, mixed)
    mixed = jnp.where(odd & (lane == 1), sums - high, mixed)
    mixed_ref[...] = mixed.astype(BF16)


def transform_kernel(message_ref, transform_ref, scratch_ref):
    half = LANES
    size = 2 * half
    scratch_ref[...] = message_ref[...].astype(F32)
    packed = scratch_ref[pl.ds(0, size, 2), :]
    extra = scratch_ref[pl.ds(1, size, 2), :]
    tri = packed[:half]
    tri_t = tri.T
    cross = packed[half:]
    row = iota((half, half), 0)
    col = iota((half, half), 1)
    first = jnp.where(row <= col, tri, tri_t)
    second = jnp.where(row > col, tri, tri_t)
    second = jnp.where(row == col, extra[:half, half // 2 : half // 2 + 1], second)
    matrix = jnp.concatenate(
        [jnp.concatenate([first, cross], axis=1), jnp.concatenate([cross.T, second], axis=1)], axis=0
    )
    same = iota((size, size), 0) == iota((size, size), 1)
    matrix = matrix + jnp.where(same, size - 1.0, 0.0)
    innovation = extra[:, 0:1] + extra[:, 1:2]
    squares = jnp.sum(jnp.sum(matrix * matrix, axis=0, keepdims=True), axis=1, keepdims=True)
    norm_scale = 0.5 * jnp.sqrt(squares)
    diagonal = jnp.where(same, 1.5, 0.0)
    root_iter = matrix / norm_scale
    correction = diagonal - 0.5 * root_iter
    inverse_iter = correction
    root_iter = dot3(split(root_iter), split(correction))
    for newton_step in range(1, NSTEPS):
        inverse_split = split(inverse_iter)
        root_split = split(root_iter)
        correction = split(diagonal - 0.5 * dot3(inverse_split, root_split))
        if newton_step < NSTEPS - 1:
            root_iter = dot3(root_split, correction)
        inverse_iter = dot3(correction, inverse_split)
    root = inverse_iter / jnp.sqrt(norm_scale)
    root_split = split(root)
    inner = dot3(root_split, split(jnp.broadcast_to(innovation, (size, LANES))))
    mean_shift = dot3(root_split, split(inner))[:, 0:1]
    transform_ref[...] = (math.sqrt(size - 1.0) * root + mean_shift).astype(BF16)


def call(kernel, shapes, *args, scratch=()):
    return pl.pallas_call(
        kernel,
        out_shape=shapes,
        in_specs=[pl.BlockSpec(memory_space=pltpu.VMEM)] * len(args),
        out_specs=jax.tree.map(lambda _: pl.BlockSpec(memory_space=pltpu.VMEM), shapes),
        scratch_shapes=scratch,
    )(*args)


def update_columns(column_block, transform):
    average = jnp.mean(column_block.astype(F32), axis=0)
    anomaly = (column_block.astype(F32) - average[None, :]).astype(BF16)
    combined = dot(transform, anomaly, ((0,), (0,)))
    return (combined + average[None, :]).astype(BF16)


def exchange(message, axes, count):
    blocks = message.reshape(count, -1, message.shape[1])
    return lax.all_to_all(blocks, axes, 0, 0, tiled=True).reshape(message.shape)


def body(ensemble, obs_anomaly, innovation, obs_precision, owner_region, neighbours):
    regions = lax.axis_size("region")
    levels = lax.axis_size("level")
    members = obs_anomaly.shape[2]
    local_obs = obs_anomaly.shape[1]
    capacity = 3 * local_obs // (2 * regions)
    size = 2 * regions * levels
    owners = owner_region.reshape(1, local_obs)
    obs = obs_anomaly[0]
    shape = jax.ShapeDtypeStruct
    rows = call(
        functools.partial(place_kernel, regions, capacity),
        shape((regions * capacity, members), BF16),
        owners,
        obs_precision,
        obs,
    )
    routed = exchange(rows, "region", regions)
    sums = call(
        innovation_kernel, shape((members, LANES), F32), owners, obs_precision, innovation, obs
    )
    high, low, wide = call(
        functools.partial(weight_kernel, regions, levels, neighbours.shape[1]),
        (shape((size, size), BF16), shape((size, size), BF16), shape((size, LANES), F32)),
        neighbours,
    )
    message = call(
        covariance_kernel,
        shape((size, LANES), BF16),
        routed,
        sums,
        scratch=[pltpu.VMEM((size, LANES), F32)],
    )
    message = exchange(message, ("region", "level"), regions * levels)
    message = call(
        functools.partial(mix_kernel, levels), shape((size, LANES), BF16), message, high, low, wide
    )
    message = exchange(message, ("region", "level"), regions * levels)
    transform = call(
        transform_kernel,
        shape((members, members), BF16),
        message,
        scratch=[pltpu.VMEM((size, LANES), F32)],
    )
    return update_columns(ensemble[0], transform)[None]


def solution(mesh):
    return jax.shard_map(
        body,
        mesh=mesh,
        in_specs=(
            P("level", None, "region"),
            P("level", "region", None),
            P("level", "region"),
            P("level", "region"),
            P("level", "region", None),
            P(),
        ),
        out_specs=P("level", None, "region"),
        check_vma=False,
    )
```

```python
import functools
import math

import jax
import jax.numpy as jnp
from jax import lax
from jax.experimental import pallas as pl
from jax.experimental.pallas import tpu as pltpu
from jax.sharding import PartitionSpec as P

NSTEPS = 4
TAPER = 0.6
DECAY = 0.5
LANES = 128
COLUMNS, PLANES, CORES = 4, 8, 2
PAIR = 2
GROUPS = PLANES // PAIR
EXTRA = 8
VMEM_LIMIT = 16 << 20
BF16 = jnp.bfloat16
F32 = jnp.float32


def iota(shape, dim):
    return lax.broadcasted_iota(jnp.int32, shape, dim)


def dot(left, right, dims=((1,), (0,))):
    return lax.dot_general(left, right, (dims, ((), ())), preferred_element_type=F32)


def split(value):
    high = value.astype(BF16)
    return high, (value - high.astype(F32)).astype(BF16)


def dot3(left, right, dims=((1,), (0,))):
    lh, ll = left
    rh, rl = right
    return dot(lh, rh, dims) + (dot(lh, rl, dims) + dot(ll, rh, dims))


def region_parts(region):
    return region // (PLANES * CORES), region // CORES % PLANES, region % CORES


def site(region):
    x, z, core = region_parts(region)
    place = (core * PAIR + z % PAIR) * COLUMNS + x
    return place * GROUPS + z // PAIR


def region_at(place, group):
    core, z, x = place // (PAIR * COLUMNS), place // COLUMNS % PAIR, place % COLUMNS
    return (x * PLANES + group * PAIR + z) * CORES + core


def weights_transposed(listed):
    neigh, regions = listed.shape
    owner = iota((regions, regions), 0)
    weight = (owner == iota((regions, regions), 1)).astype(F32)
    for place in range(neigh):
        weight = weight + TAPER ** (place + 1) * (listed[place : place + 1, :] == owner).astype(F32)
    return weight


def onehot(hit):
    return hit.astype(F32).astype(BF16)


def place_kernel(
    regions, capacity, owner_ref, precision_ref, innovation_ref, obs_ref, listed_ref, rows_ref
):
    count = owner_ref.shape[1]
    blocks = count // LANES
    region_ids = iota((regions, LANES), 0)
    earlier = iota((LANES, LANES), 0) < iota((LANES, LANES), 1)
    counter = jnp.concatenate([onehot(earlier), jnp.ones((LANES, LANES), BF16)], axis=1)
    owners = owner_ref[...]
    named = [region_ids == owners[:, b * LANES : (b + 1) * LANES] for b in range(blocks)]
    ranks = dot(jnp.concatenate([onehot(hit) for hit in named], axis=0), counter)
    base = (site(region_ids) * capacity).astype(F32)
    pieces = []
    for b in range(blocks):
        part = ranks[b * regions : (b + 1) * regions]
        slot = jnp.where(named[b], part[:, :LANES] + base, 0.0)
        pieces.append(jnp.sum(slot, axis=0, keepdims=True))
        base = base + part[:, LANES:]
    slots = jnp.concatenate(pieces, axis=1).astype(jnp.int32)
    precision = precision_ref[...].astype(F32)
    scale = jnp.sqrt(precision)
    obs = obs_ref[...]

    factor = precision * innovation_ref[...].astype(F32)
    hit = iota((regions, count), 0) == owners
    sums = split(dot(jnp.where(hit, factor, 0.0).astype(BF16), obs))
    half = obs[:, LANES:].astype(F32)
    squares = split(dot(jnp.where(hit, precision, 0.0).astype(BF16), (half * half).astype(BF16)))
    weight = split(weights_transposed(listed_ref[...]))
    sites = regions // GROUPS
    row = iota((regions, sites * EXTRA), 1)
    place, item = row // EXTRA, row % EXTRA

    def chosen(group, valid):
        pick = onehot((iota((regions, sites * EXTRA), 0) == region_at(place, group)) & valid)
        return split(dot(weight[0], pick) + dot(weight[1], pick))

    over = ((0,), (0,))
    second = (item - GROUPS) * 2
    is_diag = (item >= GROUPS) & (item < GROUPS + GROUPS // 2)
    extra = dot3(chosen(item, item < GROUPS), sums, over)
    left = dot3(chosen(second, is_diag), squares, over)
    right = dot3(chosen(second + 1, is_diag), squares, over)
    extra = (extra + jnp.concatenate([left, right], axis=1)).astype(BF16)

    span = GROUPS * capacity
    at_once = 4
    for start in range(0, sites, at_once):
        hit = slots == iota((at_once * span, count), 0) + start * span
        placed = dot(jnp.where(hit, scale, 0.0).astype(BF16), obs).astype(BF16)
        for k in range(at_once):
            at = (start + k) * (span + EXTRA)
            rows_ref[at : at + span, :] = placed[k * span : (k + 1) * span]
            rows_ref[at + span : at + span + EXTRA, :] = extra[(start + k) * EXTRA : (start + k + 1) * EXTRA]


def weight_kernel(levels, listed_ref, high_ref, low_ref):
    size, columns = high_ref.shape
    weight = split(weights_transposed(listed_ref[...]))
    regions = listed_ref.shape[1]
    expand = onehot(iota((regions, size), 0) == iota((regions, size), 1) // levels)
    rows = split(dot(weight[0], expand) + dot(weight[1], expand))
    col = iota((regions, columns), 1)
    x, z, core = region_parts(col // (levels * GROUPS))
    owner = (x * PLANES + (col % GROUPS) * PAIR + z % PAIR) * CORES + core
    spread = onehot(iota((regions, columns), 0) == owner)
    over = ((0,), (0,))
    full = dot(rows[0], spread, over) + dot(rows[1], spread, over)
    apart = jnp.abs(iota((size, columns), 0) % levels - iota((size, columns), 1) // GROUPS % levels)
    factor = jnp.zeros((size, columns), F32)
    for distance in range(levels):
        factor = jnp.where(apart == distance, DECAY**distance, factor)
    high, low = split(full * factor)
    high_ref[...] = high
    low_ref[...] = low


def covariance_kernel(capacity, rows_ref, message_ref, sums_ref, scratch_ref):
    half = LANES
    members = rows_ref.shape[2]
    above = iota((half, half), 0) <= iota((half, half), 1)
    for group in range(GROUPS):
        rows = rows_ref[:, group * capacity : (group + 1) * capacity, :].reshape(-1, members)
        total = dot(rows, rows, ((0,), (0,)))
        corner = jnp.where(above, total[:half, :half], total[half:, half:])
        packed = jnp.concatenate([corner, total[:half, half:]], axis=0)
        scratch_ref[pl.ds(group, members, GROUPS), :] = packed
    message_ref[...] = scratch_ref[...].astype(BF16)
    span = GROUPS * capacity
    sums_ref[...] = jnp.sum(rows_ref[:, span : span + EXTRA, :].astype(F32), axis=0)


def mix_kernel(message_ref, high_ref, low_ref, mixed_ref):
    message = message_ref[...]
    mixed_ref[...] = dot(high_ref[...], message) + dot(low_ref[...], message)


def transform_kernel(packed_ref, extra_ref, transform_ref):
    half = LANES
    size = 2 * half
    tri = packed_ref[:half, :]
    tri_t = tri.T
    cross = packed_ref[half:, :]
    row = iota((half, half), 0)
    col = iota((half, half), 1)
    first = jnp.where(row <= col, tri, tri_t)
    second = jnp.where(row > col, tri, tri_t)
    second = jnp.where(row == col, extra_ref[:, size:], second)
    matrix = jnp.concatenate(
        [jnp.concatenate([first, cross], axis=1), jnp.concatenate([cross.T, second], axis=1)], axis=0
    )
    same = iota((size, size), 0) == iota((size, size), 1)
    matrix = matrix + jnp.where(same, size - 1.0, 0.0)
    squares = jnp.sum(jnp.sum(matrix * matrix, axis=0, keepdims=True), axis=1, keepdims=True)
    norm_scale = 0.5 * jnp.sqrt(squares)
    diagonal = jnp.where(same, 1.5, 0.0)
    root_iter = matrix / norm_scale
    correction = diagonal - 0.5 * root_iter
    inverse_iter = correction
    root_iter = dot3(split(root_iter), split(correction))
    for newton_step in range(1, NSTEPS):
        inverse_split = split(inverse_iter)
        root_split = split(root_iter)
        correction = split(diagonal - 0.5 * dot3(inverse_split, root_split))
        if newton_step < NSTEPS - 1:
            root_iter = dot3(root_split, correction)
        inverse_iter = dot3(correction, inverse_split)
    root = inverse_iter / jnp.sqrt(norm_scale)
    root_split = split(root)
    innovation = jnp.broadcast_to(extra_ref[:, :size], (8, size))
    inner = dot3(split(innovation), root_split)
    mean_shift = dot3(split(inner), root_split)[0:1, :]
    transform_ref[...] = (math.sqrt(size - 1.0) * root + mean_shift).astype(BF16)


def call(kernel, shapes, *args, scratch=()):
    return pl.pallas_call(
        kernel,
        out_shape=shapes,
        in_specs=[pl.BlockSpec(memory_space=pltpu.VMEM)] * len(args),
        out_specs=jax.tree.map(lambda _: pl.BlockSpec(memory_space=pltpu.VMEM), shapes),
        scratch_shapes=scratch,
        compiler_params=pltpu.CompilerParams(vmem_limit_bytes=VMEM_LIMIT),
    )(*args)


def update_columns(column_block, transposed):
    average = jnp.mean(column_block.astype(F32), axis=0)
    anomaly = (column_block.astype(F32) - average[None, :]).astype(BF16)
    combined = dot(transposed, anomaly)
    return (combined + average[None, :]).astype(BF16)


def exchange(message, axes, count, groups=None):
    blocks = message.reshape(count, -1, message.shape[-1])
    return lax.all_to_all(blocks, axes, 0, 0, tiled=True, axis_index_groups=groups)


def body(ensemble, obs_anomaly, innovation, obs_precision, owner_region, neighbours):
    regions = lax.axis_size("region")
    levels = lax.axis_size("level")
    my_region = lax.axis_index("region")
    my_level = lax.axis_index("level")
    members = obs_anomaly.shape[2]
    local_obs = obs_anomaly.shape[1]
    capacity = 3 * local_obs // (2 * regions)
    places = regions // GROUPS
    devices = regions * levels
    owners = owner_region.reshape(1, local_obs)
    listed = neighbours.T
    shape = jax.ShapeDtypeStruct
    rows = call(
        functools.partial(place_kernel, regions, capacity),
        shape((places * (GROUPS * capacity + EXTRA), members), BF16),
        owners,
        obs_precision,
        innovation,
        obs_anomaly[0],
        listed,
    )
    near = [[region_at(place, group) for place in range(places)] for group in range(GROUPS)]
    routed = exchange(rows, "region", places, near)
    high, low = call(
        functools.partial(weight_kernel, levels),
        (shape((devices, devices * GROUPS), BF16), shape((devices, devices * GROUPS), BF16)),
        listed,
    )
    message, sums = call(
        functools.partial(covariance_kernel, capacity),
        (shape((members * GROUPS, LANES), BF16), shape((EXTRA, members), F32)),
        routed,
        scratch=[pltpu.VMEM((members * GROUPS, LANES), F32)],
    )
    message = exchange(message, ("region", "level"), devices).reshape(-1, LANES)

    my_group = my_region // CORES % PLANES // PAIR
    diagonals = sums[GROUPS : GROUPS + GROUPS // 2].reshape(GROUPS, LANES)
    parts = jnp.concatenate([sums[:GROUPS], diagonals], axis=1)
    part = lax.dynamic_slice_in_dim(parts, my_group, 1, 0)
    for ahead in range(1, GROUPS):
        sent = lax.dynamic_slice_in_dim(parts, (my_group + ahead) % GROUPS, 1, 0)
        pairs = []
        for region in range(regions):
            x, z, core = region_parts(region)
            pairs.append((region, (x * PLANES + (z + PAIR * ahead) % PLANES) * CORES + core))
        part = part + lax.ppermute(sent, "region", pairs)
    extra = part
    for ahead in range(1, levels):
        arrived = lax.ppermute(part, "level", [(o, (o + ahead) % levels) for o in range(levels)])
        apart = jnp.abs(my_level - (my_level - ahead) % levels)
        factor = sum(DECAY**distance * (apart == distance).astype(F32) for distance in range(levels))
        extra = extra + factor * arrived

    mixed = call(mix_kernel, shape((devices, LANES), F32), message, high, low)
    packed = exchange(mixed, ("region", "level"), devices).reshape(devices, LANES)
    transposed = call(transform_kernel, shape((members, members), BF16), packed, extra)
    return update_columns(ensemble[0], transposed)[None]


def solution(mesh):
    return jax.shard_map(
        body,
        mesh=mesh,
        in_specs=(
            P("level", None, "region"),
            P("level", "region", None),
            P("level", "region"),
            P("level", "region"),
            P("level", "region", None),
            P(),
        ),
        out_specs=P("level", None, "region"),
        check_vma=False,
    )
```

```python
import functools
import math

import jax
import jax.numpy as jnp
from jax import lax
from jax.experimental import pallas as pl
from jax.experimental.pallas import tpu as pltpu
from jax.sharding import PartitionSpec as P

NSTEPS = 4
TAPER = 0.6
DECAY = 0.5
LANES, SUBLANES = 128, 8
COLUMNS, PLANES, CORES = 4, 8, 2
PAIR = 2
GROUPS = PLANES // PAIR
EXTRA = 8
VMEM_LIMIT = 16 << 20
FIRST_LIMIT = 62 << 20
BF16 = jnp.bfloat16
F32 = jnp.float32


def iota(shape, dim):
    return lax.broadcasted_iota(jnp.int32, shape, dim)


def dot(left, right, dims=((1,), (0,))):
    return lax.dot_general(left, right, (dims, ((), ())), preferred_element_type=F32)


def split(value):
    high = value.astype(BF16)
    return high, (value - high.astype(F32)).astype(BF16)


def dot3(left, right, dims=((1,), (0,))):
    lh, ll = left
    rh, rl = right
    return dot(lh, rh, dims) + (dot(lh, rl, dims) + dot(ll, rh, dims))


def region_parts(region):
    return region // (PLANES * CORES), region // CORES % PLANES, region % CORES


def site(region):
    x, z, core = region_parts(region)
    place = (core * PAIR + z % PAIR) * COLUMNS + x
    return place * GROUPS + z // PAIR


def region_at(place, group):
    core, z, x = place // (PAIR * COLUMNS), place // COLUMNS % PAIR, place % COLUMNS
    return (x * PLANES + group * PAIR + z) * CORES + core


def weights_transposed(listed):
    neigh, regions = listed.shape
    owner = iota((regions, regions), 0)
    weight = (owner == iota((regions, regions), 1)).astype(F32)
    for place in range(neigh):
        weight = weight + TAPER ** (place + 1) * (listed[place : place + 1, :] == owner).astype(F32)
    return weight


def onehot(hit):
    return hit.astype(F32).astype(BF16)


def place_kernel(
    regions, capacity, owner_ref, precision_ref, innovation_ref, obs_ref, listed_ref, rows_ref
):
    count = owner_ref.shape[1]
    blocks = count // LANES
    region_ids = iota((regions, LANES), 0)
    earlier = iota((LANES, LANES), 0) < iota((LANES, LANES), 1)
    counter = jnp.concatenate([onehot(earlier), jnp.ones((LANES, LANES), BF16)], axis=1)
    owners = owner_ref[...]
    named = [region_ids == owners[:, b * LANES : (b + 1) * LANES] for b in range(blocks)]
    ranks = dot(jnp.concatenate([onehot(hit) for hit in named], axis=0), counter)
    base = (site(region_ids) * capacity).astype(F32)
    pieces = []
    for b in range(blocks):
        part = ranks[b * regions : (b + 1) * regions]
        slot = jnp.where(named[b], part[:, :LANES] + base, 0.0)
        pieces.append(jnp.sum(slot, axis=0, keepdims=True))
        base = base + part[:, LANES:]
    slots = jnp.concatenate(pieces, axis=1).astype(jnp.int32)
    precision = precision_ref[...].astype(F32)
    scale = jnp.sqrt(precision)
    obs = obs_ref[...]

    factor = precision * innovation_ref[...].astype(F32)
    hit = iota((regions, count), 0) == owners
    sums = split(dot(jnp.where(hit, factor, 0.0).astype(BF16), obs))
    half = obs[:, LANES:].astype(F32)
    squares = split(dot(jnp.where(hit, precision, 0.0).astype(BF16), (half * half).astype(BF16)))
    weight = split(weights_transposed(listed_ref[...]))
    sites = regions // GROUPS
    row = iota((regions, sites * EXTRA), 1)
    place, item = row // EXTRA, row % EXTRA

    def chosen(group, valid):
        pick = onehot((iota((regions, sites * EXTRA), 0) == region_at(place, group)) & valid)
        return split(dot(weight[0], pick) + dot(weight[1], pick))

    over = ((0,), (0,))
    second = (item - GROUPS) * 2
    is_diag = (item >= GROUPS) & (item < GROUPS + GROUPS // 2)
    extra = dot3(chosen(item, item < GROUPS), sums, over)
    left = dot3(chosen(second, is_diag), squares, over)
    right = dot3(chosen(second + 1, is_diag), squares, over)
    extra = (extra + jnp.concatenate([left, right], axis=1)).astype(BF16)

    span = GROUPS * capacity
    at_once = 4
    for start in range(0, sites, at_once):
        hit = slots == iota((at_once * span, count), 0) + start * span
        placed = dot(jnp.where(hit, scale, 0.0).astype(BF16), obs).astype(BF16)
        for k in range(at_once):
            at = (start + k) * (span + EXTRA)
            rows_ref[at : at + span, :] = placed[k * span : (k + 1) * span]
            rows_ref[at + span : at + span + EXTRA, :] = extra[(start + k) * EXTRA : (start + k + 1) * EXTRA]


def weight_kernel(listed_ref, high_ref, low_ref):
    size = high_ref.shape[0]
    weight = split(weights_transposed(listed_ref[...]))
    regions = listed_ref.shape[1]
    expand = onehot(iota((regions, size), 0) == iota((regions, size), 1) // SUBLANES)
    rows = split(dot(weight[0], expand) + dot(weight[1], expand))
    at = iota((regions, size), 1) // SUBLANES
    spread = onehot(iota((regions, size), 0) == region_at(at // GROUPS, at % GROUPS))
    over = ((0,), (0,))
    full = dot(rows[0], spread, over) + dot(rows[1], spread, over)
    same = iota((size, size), 0) % SUBLANES == iota((size, size), 1) % SUBLANES
    high, low = split(jnp.where(same, full, 0.0))
    high_ref[...] = high
    low_ref[...] = low


def covariance_kernel(capacity, rows_ref, message_ref, sums_ref):
    half = LANES
    members = rows_ref.shape[2]
    places = message_ref.shape[0]
    piece = members // places
    above = iota((half, half), 0) <= iota((half, half), 1)
    for group in range(GROUPS):
        rows = rows_ref[:, group * capacity : (group + 1) * capacity, :].reshape(-1, members)
        total = dot(rows, rows, ((0,), (0,)))
        corner = jnp.where(above, total[:half, :half], total[half:, half:])
        packed = jnp.concatenate([corner, total[:half, half:]], axis=0).astype(BF16)
        message_ref[:, group * piece : (group + 1) * piece, :] = packed.reshape(places, piece, LANES)
    span = GROUPS * capacity
    sums_ref[...] = jnp.sum(rows_ref[:, span : span + EXTRA, :].astype(F32), axis=0)


def mix_kernel(message_ref, high_ref, low_ref, mixed_ref):
    places, rows, _ = message_ref.shape
    regions, piece, _ = mixed_ref.shape
    message = message_ref[...].reshape(regions, piece, LANES)
    parts = [
        message[:, at : at + SUBLANES, :].reshape(regions * SUBLANES, LANES) for at in range(0, piece, SUBLANES)
    ]
    wide = jnp.concatenate(parts, axis=1)
    mixed = (dot(high_ref[...], wide) + dot(low_ref[...], wide)).astype(BF16)
    for part in range(len(parts)):
        at = part * SUBLANES
        block = mixed[:, part * LANES : (part + 1) * LANES]
        mixed_ref[:, at : at + SUBLANES, :] = block.reshape(regions, SUBLANES, LANES)


def gather_kernel(pieces_ref, extra_ref, own_ref, sent_ref):
    regions, piece, _ = pieces_ref.shape
    size = regions // GROUPS * piece
    for place in range(regions // GROUPS):
        total = pieces_ref[region_at(place, 0)].astype(F32)
        for group in range(1, GROUPS):
            total = total + pieces_ref[region_at(place, group)].astype(F32)
        own_ref[place * piece : (place + 1) * piece, :] = total
        sent_ref[place * piece : (place + 1) * piece, :] = total.astype(BF16)
    extra = extra_ref[...]
    high = extra.astype(BF16).astype(F32)
    low = extra - high
    rows = [value[:, at : at + LANES] for value in (high, low) for at in range(0, 3 * LANES, LANES)]
    rows = jnp.concatenate(rows + [jnp.zeros((2, LANES), F32)], axis=0)
    own_ref[size:, :] = rows
    sent_ref[size:, :] = rows.astype(BF16)


def transform_kernel(levels, level_ref, own_ref, *refs):
    half = LANES
    size = 2 * half
    transform_ref = refs[-1]
    level = level_ref[0]
    everything = own_ref[...]
    for ahead in range(1, levels):
        source = lax.rem(level + (levels - ahead), levels)
        apart = jnp.abs(level - source)
        factor = jnp.where(apart == 1, DECAY, jnp.where(apart == 2, DECAY**2, DECAY**3))
        everything = everything + factor * refs[ahead - 1][...].astype(F32)
    extra = everything[size : size + 3] + everything[size + 3 : size + 6]
    tri = everything[:half]
    tri_t = tri.T
    cross = everything[half:size]
    row = iota((half, half), 0)
    col = iota((half, half), 1)
    first = jnp.where(row <= col, tri, tri_t)
    second = jnp.where(row > col, tri, tri_t)
    second = jnp.where(row == col, extra[2:3], second)
    matrix = jnp.concatenate(
        [jnp.concatenate([first, cross], axis=1), jnp.concatenate([cross.T, second], axis=1)], axis=0
    )
    same = iota((size, size), 0) == iota((size, size), 1)
    matrix = matrix + jnp.where(same, size - 1.0, 0.0)
    squares = jnp.sum(jnp.sum(matrix * matrix, axis=0, keepdims=True), axis=1, keepdims=True)
    norm_scale = 0.5 * jnp.sqrt(squares)
    diagonal = jnp.where(same, 1.5, 0.0)
    root_iter = matrix / norm_scale
    correction = diagonal - 0.5 * root_iter
    inverse_iter = correction
    root_iter = dot3(split(root_iter), split(correction))
    for newton_step in range(1, NSTEPS):
        inverse_split = split(inverse_iter)
        root_split = split(root_iter)
        correction = split(diagonal - 0.5 * dot3(inverse_split, root_split))
        if newton_step < NSTEPS - 1:
            root_iter = dot3(root_split, correction)
        inverse_iter = dot3(correction, inverse_split)
    root = inverse_iter / jnp.sqrt(norm_scale)
    root_split = split(root)
    innovation = jnp.concatenate([extra[0:1], extra[1:2]], axis=1)
    innovation = jnp.broadcast_to(innovation, (SUBLANES, size))
    inner = dot3(split(innovation), root_split)
    mean_shift = dot3(split(inner), root_split)[0:1, :]
    transform_ref[...] = (math.sqrt(size - 1.0) * root + mean_shift).astype(BF16)


def call(kernel, shapes, *args, scratch=(), limit=VMEM_LIMIT, scalars=0):
    spaces = [pltpu.SMEM] * scalars + [pltpu.VMEM] * (len(args) - scalars)
    return pl.pallas_call(
        kernel,
        out_shape=shapes,
        in_specs=[pl.BlockSpec(memory_space=space) for space in spaces],
        out_specs=jax.tree.map(lambda _: pl.BlockSpec(memory_space=pltpu.VMEM), shapes),
        scratch_shapes=scratch,
        compiler_params=pltpu.CompilerParams(vmem_limit_bytes=limit),
    )(*args)


def update_columns(column_block, transposed):
    average = jnp.mean(column_block.astype(F32), axis=0)
    anomaly = (column_block.astype(F32) - average[None, :]).astype(BF16)
    combined = dot(transposed, anomaly)
    return (combined + average[None, :]).astype(BF16)


def exchange(message, axes, count, groups=None):
    blocks = message.reshape(count, -1, message.shape[-1])
    return lax.all_to_all(blocks, axes, 0, 0, tiled=True, axis_index_groups=groups)


def body(ensemble, obs_anomaly, innovation, obs_precision, owner_region, neighbours):
    regions = lax.axis_size("region")
    levels = lax.axis_size("level")
    my_region = lax.axis_index("region")
    my_level = lax.axis_index("level")
    members = obs_anomaly.shape[2]
    local_obs = obs_anomaly.shape[1]
    capacity = 3 * local_obs // (2 * regions)
    places = regions // GROUPS
    owners = owner_region.reshape(1, local_obs)
    listed = neighbours.T
    shape = jax.ShapeDtypeStruct
    rows = call(
        functools.partial(place_kernel, regions, capacity),
        shape((places * (GROUPS * capacity + EXTRA), members), BF16),
        owners,
        obs_precision,
        innovation,
        obs_anomaly[0],
        listed,
        limit=FIRST_LIMIT,
    )
    near = [[region_at(place, group) for place in range(places)] for group in range(GROUPS)]
    routed = exchange(rows, "region", places, near)
    piece = members // places
    high, low = call(
        weight_kernel, (shape((regions * SUBLANES, regions * SUBLANES), BF16),) * 2, listed
    )
    message, sums = call(
        functools.partial(covariance_kernel, capacity),
        (shape((places, GROUPS * piece, LANES), BF16), shape((EXTRA, members), F32)),
        routed,
    )
    message = lax.all_to_all(message, "region", 0, 0, tiled=True, axis_index_groups=near)
    mixed = call(mix_kernel, shape((regions, piece, LANES), BF16), message, high, low)
    mixed, sums = lax.optimization_barrier((mixed, sums))
    pieces = lax.all_to_all(mixed, "region", 0, 0, tiled=True)

    my_group = my_region // CORES % PLANES // PAIR
    diagonals = sums[GROUPS : GROUPS + GROUPS // 2].reshape(GROUPS, LANES)
    parts = jnp.concatenate([sums[:GROUPS], diagonals], axis=1)
    part = lax.dynamic_slice_in_dim(parts, my_group, 1, 0)
    for ahead in range(1, GROUPS):
        sent = lax.dynamic_slice_in_dim(parts, (my_group + ahead) % GROUPS, 1, 0)
        pairs = []
        for region in range(regions):
            x, z, core = region_parts(region)
            pairs.append((region, (x * PLANES + (z + PAIR * ahead) % PLANES) * CORES + core))
        part = part + lax.ppermute(sent, "region", pairs)

    height = members + SUBLANES
    own, sent = call(
        gather_kernel, (shape((height, LANES), F32), shape((height, LANES), BF16)), pieces, part
    )
    arrived = [
        lax.ppermute(sent, "level", [(o, (o + ahead) % levels) for o in range(levels)])
        for ahead in range(1, levels)
    ]
    transposed = call(
        functools.partial(transform_kernel, levels),
        shape((members, members), BF16),
        my_level.astype(jnp.int32).reshape(1),
        own,
        *arrived,
        scalars=1,
    )
    return update_columns(ensemble[0], transposed)[None]


def solution(mesh):
    return jax.shard_map(
        body,
        mesh=mesh,
        in_specs=(
            P("level", None, "region"),
            P("level", "region", None),
            P("level", "region"),
            P("level", "region"),
            P("level", "region", None),
            P(),
        ),
        out_specs=P("level", None, "region"),
        check_vma=False,
    )
```

```python
import functools
import math

import jax
import jax.numpy as jnp
from jax import lax
from jax.experimental import pallas as pl
from jax.experimental.pallas import tpu as pltpu
from jax.sharding import PartitionSpec as P

NSTEPS = 4
TAPER = 0.6
DECAY = 0.5
LANES, SUBLANES = 128, 8
COLUMNS, PLANES, CORES = 4, 8, 2
PAIR = 2
GROUPS = PLANES // PAIR
WIDTH = 512
EXTRA = 8
VMEM_LIMIT = 16 << 20
FIRST_LIMIT = 62 << 20
BF16 = jnp.bfloat16
F32 = jnp.float32


def iota(shape, dim):
    return lax.broadcasted_iota(jnp.int32, shape, dim)


def dot(left, right, dims=((1,), (0,))):
    return lax.dot_general(left, right, (dims, ((), ())), preferred_element_type=F32)


def split(value):
    high = value.astype(BF16)
    return high, (value - high.astype(F32)).astype(BF16)


def dot3(left, right, dims=((1,), (0,))):
    lh, ll = left
    rh, rl = right
    return dot(lh, rh, dims) + (dot(lh, rl, dims) + dot(ll, rh, dims))


def region_parts(region):
    return region // (PLANES * CORES), region // CORES % PLANES, region % CORES


def site(region):
    x, z, core = region_parts(region)
    place = (core * PAIR + z % PAIR) * COLUMNS + x
    return place * GROUPS + z // PAIR


def region_at(place, group):
    core, z, x = place // (PAIR * COLUMNS), place // COLUMNS % PAIR, place % COLUMNS
    return (x * PLANES + group * PAIR + z) * CORES + core


def weights_transposed(listed):
    neigh, regions = listed.shape
    owner = iota((regions, regions), 0)
    weight = (owner == iota((regions, regions), 1)).astype(F32)
    for place in range(neigh):
        weight = weight + TAPER ** (place + 1) * (listed[place : place + 1, :] == owner).astype(F32)
    return weight


def onehot(hit):
    return hit.astype(F32).astype(BF16)


def place_kernel(
    regions, capacity, owner_ref, precision_ref, innovation_ref, obs_ref, listed_ref, rows_ref
):
    count = owner_ref.shape[1]
    blocks = count // LANES
    region_ids = iota((regions, LANES), 0)
    earlier = iota((LANES, LANES), 0) < iota((LANES, LANES), 1)
    counter = jnp.concatenate([onehot(earlier), jnp.ones((LANES, LANES), BF16)], axis=1)
    owners = owner_ref[...]
    named = [region_ids == owners[:, b * LANES : (b + 1) * LANES] for b in range(blocks)]
    ranks = dot(jnp.concatenate([onehot(hit) for hit in named], axis=0), counter)
    base = (site(region_ids) * capacity).astype(F32)
    pieces = []
    for b in range(blocks):
        part = ranks[b * regions : (b + 1) * regions]
        slot = jnp.where(named[b], part[:, :LANES] + base, 0.0)
        pieces.append(jnp.sum(slot, axis=0, keepdims=True))
        base = base + part[:, LANES:]
    slots = jnp.concatenate(pieces, axis=1).astype(jnp.int32)
    precision = precision_ref[...].astype(F32)
    scale = jnp.sqrt(precision)
    obs = obs_ref[...]

    factor = precision * innovation_ref[...].astype(F32)
    hit = iota((regions, count), 0) == owners
    sums = split(dot(jnp.where(hit, factor, 0.0).astype(BF16), obs))
    half = obs[:, LANES:].astype(F32)
    squares = split(dot(jnp.where(hit, precision, 0.0).astype(BF16), (half * half).astype(BF16)))
    weight = split(weights_transposed(listed_ref[...]))
    sites = regions // GROUPS
    row = iota((regions, sites * EXTRA), 1)
    place, item = row // EXTRA, row % EXTRA

    def chosen(group, valid):
        pick = onehot((iota((regions, sites * EXTRA), 0) == region_at(place, group)) & valid)
        return split(dot(weight[0], pick) + dot(weight[1], pick))

    over = ((0,), (0,))
    second = (item - GROUPS) * 2
    is_diag = (item >= GROUPS) & (item < GROUPS + GROUPS // 2)
    extra = dot3(chosen(item, item < GROUPS), sums, over)
    left = dot3(chosen(second, is_diag), squares, over)
    right = dot3(chosen(second + 1, is_diag), squares, over)
    extra = (extra + jnp.concatenate([left, right], axis=1)).astype(BF16)

    span = GROUPS * capacity
    at_once = 4
    for start in range(0, sites, at_once):
        hit = slots == iota((at_once * span, count), 0) + start * span
        placed = dot(jnp.where(hit, scale, 0.0).astype(BF16), obs).astype(BF16)
        for k in range(at_once):
            at = (start + k) * (span + EXTRA)
            rows_ref[at : at + span, :] = placed[k * span : (k + 1) * span]
            rows_ref[at + span : at + span + EXTRA, :] = extra[(start + k) * EXTRA : (start + k + 1) * EXTRA]


def weight_kernel(listed_ref, high_ref, low_ref):
    size = high_ref.shape[0]
    weight = split(weights_transposed(listed_ref[...]))
    regions = listed_ref.shape[1]
    expand = onehot(iota((regions, size), 0) == iota((regions, size), 1) // SUBLANES)
    rows = split(dot(weight[0], expand) + dot(weight[1], expand))
    at = iota((regions, size), 1) // SUBLANES
    spread = onehot(iota((regions, size), 0) == region_at(at // GROUPS, at % GROUPS))
    over = ((0,), (0,))
    full = dot(rows[0], spread, over) + dot(rows[1], spread, over)
    same = iota((size, size), 0) % SUBLANES == iota((size, size), 1) % SUBLANES
    high, low = split(jnp.where(same, full, 0.0))
    high_ref[...] = high
    low_ref[...] = low


def covariance_kernel(capacity, rows_ref, message_ref, sums_ref):
    half = LANES
    members = rows_ref.shape[2]
    places = message_ref.shape[0]
    piece = members // places
    above = iota((half, half), 0) <= iota((half, half), 1)
    for group in range(GROUPS):
        rows = rows_ref[:, group * capacity : (group + 1) * capacity, :].reshape(-1, members)
        total = dot(rows, rows, ((0,), (0,)))
        corner = jnp.where(above, total[:half, :half], total[half:, half:])
        packed = jnp.concatenate([corner, total[:half, half:]], axis=0).astype(BF16)
        message_ref[:, group * piece : (group + 1) * piece, :] = packed.reshape(places, piece, LANES)
    span = GROUPS * capacity
    sums = jnp.sum(rows_ref[:, span : span + EXTRA, :].astype(F32), axis=0)
    for group in range(GROUPS):
        at, inner = GROUPS + group // 2, group % 2
        diagonal = sums[at : at + 1, inner * half : (inner + 1) * half]
        row = jnp.concatenate([sums[group : group + 1], diagonal], axis=1)
        sums_ref[group // 2, inner : inner + 1, :] = row


def mix_kernel(message_ref, high_ref, low_ref, mixed_ref):
    places, rows, _ = message_ref.shape
    regions, piece, _ = mixed_ref.shape
    message = message_ref[...].reshape(regions, piece, LANES)
    parts = [
        message[:, at : at + SUBLANES, :].reshape(regions * SUBLANES, LANES) for at in range(0, piece, SUBLANES)
    ]
    wide = jnp.concatenate(parts, axis=1)
    mixed = (dot(high_ref[...], wide) + dot(low_ref[...], wide)).astype(BF16)
    for part in range(len(parts)):
        at = part * SUBLANES
        block = mixed[:, part * LANES : (part + 1) * LANES]
        mixed_ref[:, at : at + SUBLANES, :] = block.reshape(regions, SUBLANES, LANES)


def gather_kernel(pieces_ref, extra_ref, own_ref, sent_ref):
    regions, piece, _ = pieces_ref.shape
    size = regions // GROUPS * piece
    for place in range(regions // GROUPS):
        total = pieces_ref[region_at(place, 0)].astype(F32)
        for group in range(1, GROUPS):
            total = total + pieces_ref[region_at(place, group)].astype(F32)
        own_ref[place * piece : (place + 1) * piece, :] = total
        sent_ref[place * piece : (place + 1) * piece, :] = total.astype(BF16)
    extra = extra_ref[...]
    high = extra.astype(BF16).astype(F32)
    low = extra - high
    rows = [value[:, at : at + LANES] for value in (high, low) for at in range(0, 3 * LANES, LANES)]
    rows = jnp.concatenate(rows + [jnp.zeros((2, LANES), F32)], axis=0)
    own_ref[size:, :] = rows
    sent_ref[size:, :] = rows.astype(BF16)


def anomaly_kernel(ensemble_ref, average_ref, anomaly_ref):
    members, columns = ensemble_ref.shape
    for at in range(0, columns, WIDTH):
        block = ensemble_ref[:, at : at + WIDTH].astype(F32)
        average = jnp.sum(block, axis=0, keepdims=True) * (1.0 / members)
        average_ref[:, at : at + WIDTH] = average
        anomaly_ref[:, at : at + WIDTH] = (block - average).astype(BF16)


def transform_kernel(levels, level_ref, average_ref, anomaly_ref, own_ref, *refs):
    half = LANES
    size = 2 * half
    output_ref, block_ref, semaphores = refs[-3:]
    level = level_ref[0]
    everything = own_ref[...]
    for ahead in range(1, levels):
        source = lax.rem(level + (levels - ahead), levels)
        apart = jnp.abs(level - source)
        factor = jnp.where(apart == 1, DECAY, jnp.where(apart == 2, DECAY**2, DECAY**3))
        everything = everything + factor * refs[ahead - 1][...].astype(F32)
    extra = everything[size : size + 3] + everything[size + 3 : size + 6]
    tri = everything[:half]
    tri_t = tri.T
    cross = everything[half:size]
    row = iota((half, half), 0)
    col = iota((half, half), 1)
    first = jnp.where(row <= col, tri, tri_t)
    second = jnp.where(row > col, tri, tri_t)
    second = jnp.where(row == col, extra[2:3], second)
    matrix = jnp.concatenate(
        [jnp.concatenate([first, cross], axis=1), jnp.concatenate([cross.T, second], axis=1)], axis=0
    )
    same = iota((size, size), 0) == iota((size, size), 1)
    matrix = matrix + jnp.where(same, size - 1.0, 0.0)
    squares = jnp.sum(jnp.sum(matrix * matrix, axis=0, keepdims=True), axis=1, keepdims=True)
    norm_scale = 0.5 * jnp.sqrt(squares)
    diagonal = jnp.where(same, 1.5, 0.0)
    root_iter = matrix / norm_scale
    correction = diagonal - 0.5 * root_iter
    inverse_iter = correction
    root_iter = dot3(split(root_iter), split(correction))
    for newton_step in range(1, NSTEPS):
        inverse_split = split(inverse_iter)
        root_split = split(root_iter)
        correction = split(diagonal - 0.5 * dot3(inverse_split, root_split))
        if newton_step < NSTEPS - 1:
            root_iter = dot3(root_split, correction)
        inverse_iter = dot3(correction, inverse_split)
    root = inverse_iter / jnp.sqrt(norm_scale)
    root_split = split(root)
    innovation = jnp.concatenate([extra[0:1], extra[1:2]], axis=1)
    innovation = jnp.broadcast_to(innovation, (SUBLANES, size))
    inner = dot3(split(innovation), root_split)
    mean_shift = dot3(split(inner), root_split)[0:1, :]
    transform = (math.sqrt(size - 1.0) * root + mean_shift).astype(BF16)
    copies = []
    for step, at in enumerate(range(0, anomaly_ref.shape[1], WIDTH)):
        span = slice(at, at + WIDTH)
        combined = dot(transform, anomaly_ref[:, span]) + average_ref[:, span]
        block_ref[:, span] = combined.astype(BF16)
        copy = pltpu.make_async_copy(
            block_ref.at[:, span], output_ref.at[:, span], semaphores.at[step]
        )
        copy.start()
        copies.append(copy)
    for copy in copies:
        copy.wait()


def call(kernel, shapes, *args, scratch=(), limit=VMEM_LIMIT, scalars=0, space=pltpu.VMEM):
    spaces = [pltpu.SMEM] * scalars + [pltpu.VMEM] * (len(args) - scalars)
    return pl.pallas_call(
        kernel,
        out_shape=shapes,
        in_specs=[pl.BlockSpec(memory_space=where) for where in spaces],
        out_specs=jax.tree.map(lambda _: pl.BlockSpec(memory_space=space), shapes),
        scratch_shapes=scratch,
        compiler_params=pltpu.CompilerParams(vmem_limit_bytes=limit),
    )(*args)


def exchange(message, axes, count, groups=None):
    blocks = message.reshape(count, -1, message.shape[-1])
    return lax.all_to_all(blocks, axes, 0, 0, tiled=True, axis_index_groups=groups)


def body(ensemble, obs_anomaly, innovation, obs_precision, owner_region, neighbours):
    regions = lax.axis_size("region")
    levels = lax.axis_size("level")
    my_region = lax.axis_index("region")
    my_level = lax.axis_index("level")
    members = obs_anomaly.shape[2]
    local_obs = obs_anomaly.shape[1]
    capacity = 3 * local_obs // (2 * regions)
    places = regions // GROUPS
    owners = owner_region.reshape(1, local_obs)
    listed = neighbours.T
    shape = jax.ShapeDtypeStruct
    rows = call(
        functools.partial(place_kernel, regions, capacity),
        shape((places * (GROUPS * capacity + EXTRA), members), BF16),
        owners,
        obs_precision,
        innovation,
        obs_anomaly[0],
        listed,
        limit=FIRST_LIMIT,
    )
    near = [[region_at(place, group) for place in range(places)] for group in range(GROUPS)]
    routed = exchange(rows, "region", places, near)
    piece = members // places
    high, low = call(
        weight_kernel, (shape((regions * SUBLANES, regions * SUBLANES), BF16),) * 2, listed
    )
    message, sums = call(
        functools.partial(covariance_kernel, capacity),
        (shape((places, GROUPS * piece, LANES), BF16), shape((2, GROUPS // 2, members + LANES), F32)),
        routed,
    )
    message = lax.all_to_all(message, "region", 0, 0, tiled=True, axis_index_groups=near)

    def other_group(step):
        pairs = []
        for region in range(regions):
            x, z, core = region_parts(region)
            pairs.append((region, (x * PLANES + (z ^ (step * PAIR))) * CORES + core))
        return pairs

    my_group = my_region // CORES % PLANES // PAIR
    near_half, in_half = my_group // 2, my_group % 2
    swapped = lax.ppermute(
        lax.dynamic_index_in_dim(sums, 1 - near_half, 0, keepdims=False), "region", other_group(2)
    )
    kept = lax.dynamic_index_in_dim(sums, near_half, 0, keepdims=False) + swapped
    mixed = call(mix_kernel, shape((regions, piece, LANES), BF16), message, high, low)
    mixed, kept = lax.optimization_barrier((mixed, kept))
    pieces = lax.all_to_all(mixed, "region", 0, 0, tiled=True)
    swapped = lax.ppermute(
        lax.dynamic_slice_in_dim(kept, 1 - in_half, 1, 0), "region", other_group(1)
    )
    part = lax.dynamic_slice_in_dim(kept, in_half, 1, 0) + swapped

    height = members + SUBLANES
    own, sent = call(
        gather_kernel, (shape((height, LANES), F32), shape((height, LANES), BF16)), pieces, part
    )
    arrived = [
        lax.ppermute(sent, "level", [(o, (o + ahead) % levels) for o in range(levels)])
        for ahead in range(1, levels)
    ]
    columns = ensemble.shape[2]
    average, anomaly = call(
        anomaly_kernel, (shape((1, columns), F32), shape((members, columns), BF16)), ensemble[0]
    )
    analysis = call(
        functools.partial(transform_kernel, levels),
        shape((members, columns), BF16),
        my_level.astype(jnp.int32).reshape(1),
        average,
        anomaly,
        own,
        *arrived,
        scalars=1,
        space=pl.ANY,
        scratch=[
            pltpu.VMEM((members, columns), BF16),
            pltpu.SemaphoreType.DMA((columns // WIDTH,)),
        ],
    )
    return analysis[None]


def solution(mesh):
    return jax.shard_map(
        body,
        mesh=mesh,
        in_specs=(
            P("level", None, "region"),
            P("level", "region", None),
            P("level", "region"),
            P("level", "region"),
            P("level", "region", None),
            P(),
        ),
        out_specs=P("level", None, "region"),
        check_vma=False,
    )
```

```python
import functools
import math

import jax
import jax.numpy as jnp
from jax import lax
from jax.experimental import pallas as pl
from jax.experimental.pallas import tpu as pltpu
from jax.sharding import PartitionSpec as P


NSTEPS = 4
TAPER = 0.6
DECAY = 0.5
LANES, SUBLANES = 128, 8
COLUMNS, PLANES, CORES = 4, 8, 2
PAIR = 2
GROUPS = PLANES // PAIR
WIDTH = 512
EXTRA = 8
VMEM_LIMIT = 16 << 20
FIRST_LIMIT = 62 << 20
BF16 = jnp.bfloat16
F32 = jnp.float32


def iota(shape, dim):
    return lax.broadcasted_iota(jnp.int32, shape, dim)


def dot(left, right, dims=((1,), (0,))):
    return lax.dot_general(left, right, (dims, ((), ())), preferred_element_type=F32)


def split(value):
    high = value.astype(BF16)
    return high, (value - high.astype(F32)).astype(BF16)


def dot3(left, right, dims=((1,), (0,))):
    lh, ll = left
    rh, rl = right
    return dot(lh, rh, dims) + (dot(lh, rl, dims) + dot(ll, rh, dims))


def region_parts(region):
    return region // (PLANES * CORES), region // CORES % PLANES, region % CORES


def site(region):
    x, z, core = region_parts(region)
    place = (core * PAIR + z % PAIR) * COLUMNS + x
    return place * GROUPS + z // PAIR


def region_at(place, group):
    core, z, x = place // (PAIR * COLUMNS), place // COLUMNS % PAIR, place % COLUMNS
    return (x * PLANES + group * PAIR + z) * CORES + core


def weights_transposed(listed):
    neigh, regions = listed.shape
    owner = iota((regions, regions), 0)
    weight = (owner == iota((regions, regions), 1)).astype(F32)
    for place in range(neigh):
        weight = weight + TAPER ** (place + 1) * (listed[place : place + 1, :] == owner).astype(F32)
    return weight


def onehot(hit):
    return hit.astype(F32).astype(BF16)


def place_kernel(
    regions, capacity, owner_ref, precision_ref, innovation_ref, obs_ref, listed_ref, rows_ref
):
    count = owner_ref.shape[1]
    blocks = count // LANES
    region_ids = iota((regions, LANES), 0)
    earlier = iota((LANES, LANES), 0) < iota((LANES, LANES), 1)
    counter = jnp.concatenate([onehot(earlier), jnp.ones((LANES, LANES), BF16)], axis=1)
    owners = owner_ref[...]
    named = [region_ids == owners[:, b * LANES : (b + 1) * LANES] for b in range(blocks)]
    ranks = dot(jnp.concatenate([onehot(hit) for hit in named], axis=0), counter)
    base = (site(region_ids) * capacity).astype(F32)
    pieces = []
    for b in range(blocks):
        part = ranks[b * regions : (b + 1) * regions]
        slot = jnp.where(named[b], part[:, :LANES] + base, 0.0)
        pieces.append(jnp.sum(slot, axis=0, keepdims=True))
        base = base + part[:, LANES:]
    slots = jnp.concatenate(pieces, axis=1).astype(jnp.int32)
    precision = precision_ref[...].astype(F32)
    scale = jnp.sqrt(precision)
    obs = obs_ref[...]

    factor = precision * innovation_ref[...].astype(F32)
    hit = iota((regions, count), 0) == owners
    sums = split(dot(jnp.where(hit, factor, 0.0).astype(BF16), obs))
    half = obs[:, LANES:].astype(F32)
    squares = split(dot(jnp.where(hit, precision, 0.0).astype(BF16), (half * half).astype(BF16)))
    weight = split(weights_transposed(listed_ref[...]))
    sites = regions // GROUPS
    row = iota((regions, sites * EXTRA), 1)
    place, item = row // EXTRA, row % EXTRA

    def chosen(group, valid):
        pick = onehot((iota((regions, sites * EXTRA), 0) == region_at(place, group)) & valid)
        return split(dot(weight[0], pick) + dot(weight[1], pick))

    over = ((0,), (0,))
    second = (item - GROUPS) * 2
    is_diag = (item >= GROUPS) & (item < GROUPS + GROUPS // 2)
    extra = dot3(chosen(item, item < GROUPS), sums, over)
    left = dot3(chosen(second, is_diag), squares, over)
    right = dot3(chosen(second + 1, is_diag), squares, over)
    extra = (extra + jnp.concatenate([left, right], axis=1)).astype(BF16)

    span = GROUPS * capacity
    at_once = 4
    for start in range(0, sites, at_once):
        hit = slots == iota((at_once * span, count), 0) + start * span
        placed = dot(jnp.where(hit, scale, 0.0).astype(BF16), obs).astype(BF16)
        for k in range(at_once):
            at = (start + k) * (span + EXTRA)
            rows_ref[at : at + span, :] = placed[k * span : (k + 1) * span]
            rows_ref[at + span : at + span + EXTRA, :] = extra[(start + k) * EXTRA : (start + k + 1) * EXTRA]


def weight_kernel(listed_ref, high_ref, low_ref):
    size = high_ref.shape[0]
    weight = split(weights_transposed(listed_ref[...]))
    regions = listed_ref.shape[1]
    expand = onehot(iota((regions, size), 0) == iota((regions, size), 1) // SUBLANES)
    rows = split(dot(weight[0], expand) + dot(weight[1], expand))
    at = iota((regions, size), 1) // SUBLANES
    spread = onehot(iota((regions, size), 0) == region_at(at // GROUPS, at % GROUPS))
    over = ((0,), (0,))
    full = dot(rows[0], spread, over) + dot(rows[1], spread, over)
    same = iota((size, size), 0) % SUBLANES == iota((size, size), 1) % SUBLANES
    high, low = split(jnp.where(same, full, 0.0))
    high_ref[...] = high
    low_ref[...] = low


def covariance_kernel(capacity, rows_ref, message_ref, sums_ref):
    half = LANES
    members = rows_ref.shape[2]
    places = message_ref.shape[0]
    piece = members // places
    above = iota((half, half), 0) <= iota((half, half), 1)
    for group in range(GROUPS):
        rows = rows_ref[:, group * capacity : (group + 1) * capacity, :].reshape(-1, members)
        total = dot(rows, rows, ((0,), (0,)))
        corner = jnp.where(above, total[:half, :half], total[half:, half:])
        packed = jnp.concatenate([corner, total[:half, half:]], axis=0).astype(BF16)
        message_ref[:, group * piece : (group + 1) * piece, :] = packed.reshape(places, piece, LANES)
    span = GROUPS * capacity
    sums = jnp.sum(rows_ref[:, span : span + EXTRA, :].astype(F32), axis=0)
    for group in range(GROUPS):
        at, inner = GROUPS + group // 2, group % 2
        diagonal = sums[at : at + 1, inner * half : (inner + 1) * half]
        row = jnp.concatenate([sums[group : group + 1], diagonal], axis=1)
        sums_ref[group : group + 1, :] = row


def mix_kernel(message_ref, high_ref, low_ref, mixed_ref):
    regions, piece, _ = mixed_ref.shape
    message = message_ref[...].reshape(regions, piece, LANES)
    parts = [
        message[:, at : at + SUBLANES, :].reshape(regions * SUBLANES, LANES) for at in range(0, piece, SUBLANES)
    ]
    wide = jnp.concatenate(parts, axis=1)
    mixed = (dot(high_ref[...], wide) + dot(low_ref[...], wide)).astype(BF16)
    for part in range(len(parts)):
        at = part * SUBLANES
        block = mixed[:, part * LANES : (part + 1) * LANES]
        mixed_ref[:, at : at + SUBLANES, :] = block.reshape(regions, SUBLANES, LANES)


def gather_kernel(pieces_ref, own_ref, sent_ref):
    regions, piece, _ = pieces_ref.shape
    for place in range(regions // GROUPS):
        total = pieces_ref[region_at(place, 0)].astype(F32)
        for group in range(1, GROUPS):
            total = total + pieces_ref[region_at(place, group)].astype(F32)
        own_ref[place * piece : (place + 1) * piece, :] = total
        sent_ref[place * piece : (place + 1) * piece, :] = total.astype(BF16)


def anomaly_kernel(ensemble_ref, average_ref, anomaly_ref):
    members, columns = ensemble_ref.shape
    for at in range(0, columns, WIDTH):
        block = ensemble_ref[:, at : at + WIDTH].astype(F32)
        average = jnp.sum(block, axis=0, keepdims=True) * (1.0 / members)
        average_ref[:, at : at + WIDTH] = average
        anomaly_ref[:, at : at + WIDTH] = (block - average).astype(BF16)


def transform_kernel(levels, level_ref, average_ref, anomaly_ref, own_ref, extra_ref, *refs):
    half = LANES
    size = 2 * half
    output_ref, block_ref, semaphores = refs[-3:]
    level = level_ref[0]
    everything = own_ref[...]
    for ahead in range(1, levels):
        source = lax.rem(level + (levels - ahead), levels)
        apart = jnp.abs(level - source)
        factor = jnp.where(apart == 1, DECAY, jnp.where(apart == 2, DECAY**2, DECAY**3))
        everything = everything + factor * refs[ahead - 1][...].astype(F32)
    extra = extra_ref[...]
    tri = everything[:half]
    tri_t = tri.T
    cross = everything[half:size]
    row = iota((half, half), 0)
    col = iota((half, half), 1)
    first = jnp.where(row <= col, tri, tri_t)
    second = jnp.where(row > col, tri, tri_t)
    second = jnp.where(row == col, extra[:, size:], second)
    matrix = jnp.concatenate(
        [jnp.concatenate([first, cross], axis=1), jnp.concatenate([cross.T, second], axis=1)], axis=0
    )
    same = iota((size, size), 0) == iota((size, size), 1)
    matrix = matrix + jnp.where(same, size - 1.0, 0.0)
    squares = jnp.sum(jnp.sum(matrix * matrix, axis=0, keepdims=True), axis=1, keepdims=True)
    norm_scale = 0.5 * jnp.sqrt(squares)
    diagonal = jnp.where(same, 1.5, 0.0)
    root_iter = matrix / norm_scale
    correction = diagonal - 0.5 * root_iter
    inverse_iter = correction
    root_iter = dot3(split(root_iter), split(correction))
    for newton_step in range(1, NSTEPS):
        inverse_split = split(inverse_iter)
        root_split = split(root_iter)
        correction = split(diagonal - 0.5 * dot3(inverse_split, root_split))
        if newton_step < NSTEPS - 1:
            root_iter = dot3(root_split, correction)
        inverse_iter = dot3(correction, inverse_split)
    root = inverse_iter / jnp.sqrt(norm_scale)
    root_split = split(root)
    innovation = jnp.broadcast_to(extra[:, :size], (SUBLANES, size))
    inner = dot3(split(innovation), root_split)
    mean_shift = dot3(split(inner), root_split)[0:1, :]
    transform = (math.sqrt(size - 1.0) * root + mean_shift).astype(BF16)
    copies = []
    for step, at in enumerate(range(0, anomaly_ref.shape[1], WIDTH)):
        span = slice(at, at + WIDTH)
        combined = dot(transform, anomaly_ref[:, span]) + average_ref[:, span]
        block_ref[:, span] = combined.astype(BF16)
        copy = pltpu.make_async_copy(
            block_ref.at[:, span], output_ref.at[:, span], semaphores.at[step]
        )
        copy.start()
        copies.append(copy)
    for copy in copies:
        copy.wait()


def call(kernel, shapes, *args, scratch=(), limit=VMEM_LIMIT, scalars=0, space=pltpu.VMEM):
    spaces = [pltpu.SMEM] * scalars + [pltpu.VMEM] * (len(args) - scalars)
    return pl.pallas_call(
        kernel,
        out_shape=shapes,
        in_specs=[pl.BlockSpec(memory_space=where) for where in spaces],
        out_specs=jax.tree.map(lambda _: pl.BlockSpec(memory_space=space), shapes),
        scratch_shapes=scratch,
        compiler_params=pltpu.CompilerParams(vmem_limit_bytes=limit),
    )(*args)


def level_pairs(levels, ahead):
    return [(level, (level + ahead) % levels) for level in range(levels)]


def exchange(message, axes, count, groups=None):
    blocks = message.reshape(count, -1, message.shape[-1])
    return lax.all_to_all(blocks, axes, 0, 0, tiled=True, axis_index_groups=groups)


def step(ensemble, obs_anomaly, innovation, obs_precision, owner_region, neighbours):
    regions = lax.axis_size("region")
    levels = lax.axis_size("level")
    my_region = lax.axis_index("region")
    my_level = lax.axis_index("level")
    members = obs_anomaly.shape[2]
    local_obs = obs_anomaly.shape[1]
    capacity = 3 * local_obs // (2 * regions)
    places = regions // GROUPS
    owners = owner_region.reshape(1, local_obs)
    listed = neighbours.T
    shape = jax.ShapeDtypeStruct
    rows = call(
        functools.partial(place_kernel, regions, capacity),
        shape((places * (GROUPS * capacity + EXTRA), members), BF16),
        owners,
        obs_precision,
        innovation,
        obs_anomaly[0],
        listed,
        limit=FIRST_LIMIT,
    )
    near = [[region_at(place, group) for place in range(places)] for group in range(GROUPS)]
    routed = exchange(rows, "region", places, near)
    piece = members // places
    high, low = call(
        weight_kernel, (shape((regions * SUBLANES, regions * SUBLANES), BF16),) * 2, listed
    )
    message, sums = call(
        functools.partial(covariance_kernel, capacity),
        (shape((places, GROUPS * piece, LANES), BF16), shape((GROUPS, members + LANES), F32)),
        routed,
    )
    message = lax.all_to_all(message, "region", 0, 0, tiled=True, axis_index_groups=near)

    mixed = call(mix_kernel, shape((regions, piece, LANES), BF16), message, high, low)
    mixed, sums = lax.optimization_barrier((mixed, sums))
    pieces = lax.all_to_all(mixed, "region", 0, 0, tiled=True)
    parts = sums
    for ahead in range(1, levels):
        arrived = lax.ppermute(sums, "level", level_pairs(levels, ahead))
        apart = jnp.abs(my_level - (my_level - ahead) % levels)
        factor = sum(DECAY**distance * (apart == distance).astype(F32) for distance in range(levels))
        parts = parts + factor * arrived

    own, sent = call(
        gather_kernel, (shape((members, LANES), F32), shape((members, LANES), BF16)), pieces
    )
    sent, parts = lax.optimization_barrier((sent, parts))
    arrived = [
        lax.ppermute(sent, "level", level_pairs(levels, ahead)) for ahead in range(1, levels)
    ]
    my_group = my_region // CORES % PLANES // PAIR
    extra = lax.dynamic_slice_in_dim(parts, my_group, 1, 0)
    for ahead in range(1, GROUPS):
        pairs = []
        for region in range(regions):
            x, z, core = region_parts(region)
            pairs.append((region, (x * PLANES + (z + PAIR * ahead) % PLANES) * CORES + core))
        part = lax.dynamic_slice_in_dim(parts, (my_group + ahead) % GROUPS, 1, 0)
        arrived_part = lax.ppermute(part, "region", pairs)
        extra = extra + arrived_part
    columns = ensemble.shape[2]
    average, anomaly = call(anomaly_kernel, (shape((1, columns), F32), shape((members, columns), BF16)), ensemble[0])
    analysis = call(
        functools.partial(transform_kernel, levels),
        shape((members, columns), BF16),
        my_level.astype(jnp.int32).reshape(1),
        average,
        anomaly,
        own,
        extra,
        *arrived,
        scalars=1,
        space=pl.ANY,
        scratch=[
            pltpu.VMEM((members, columns), BF16),
            pltpu.SemaphoreType.DMA((columns // WIDTH,)),
        ],
    )
    return analysis[None]


def solution(mesh):
    return jax.shard_map(
        step,
        mesh=mesh,
        in_specs=(
            P("level", None, "region"),
            P("level", "region", None),
            P("level", "region"),
            P("level", "region"),
            P("level", "region", None),
            P(),
        ),
        out_specs=P("level", None, "region"),
        check_vma=False,
    )
```

```python
import functools
import math

import jax
import jax.numpy as jnp
from jax import lax
from jax.experimental import pallas as pl
from jax.experimental.pallas import tpu as pltpu
from jax.sharding import PartitionSpec as P

NSTEPS = 4
TAPER = 0.6
DECAY = 0.5
LANES, SUBLANES = 128, 8
COLUMNS, PLANES, CORES = 4, 8, 2
PAIR = 2
GROUPS = PLANES // PAIR
WIDTH = 512
EXTRA = 8
VMEM_LIMIT = 16 << 20
FIRST_LIMIT = 62 << 20
BF16 = jnp.bfloat16
F32 = jnp.float32


def iota(shape, dim):
    return lax.broadcasted_iota(jnp.int32, shape, dim)


def dot(left, right, dims=((1,), (0,))):
    return lax.dot_general(left, right, (dims, ((), ())), preferred_element_type=F32)


def split(value):
    high = value.astype(BF16)
    return high, (value - high.astype(F32)).astype(BF16)


def dot3(left, right, dims=((1,), (0,)), halves=False):
    lh, ll = left
    rh, rl = right
    if dims != ((1,), (0,)):
        return dot(lh, rh, dims) + (dot(lh, rl, dims) + dot(ll, rh, dims))
    left = jnp.concatenate([lh, lh, ll], axis=1)
    right = jnp.concatenate([rh, rl, rh], axis=0)
    half = left.shape[0] // 2
    if halves and half >= LANES:
        return jnp.concatenate([dot(left[:half], right), dot(left[half:], right)], axis=0)
    return dot(left, right)


def region_parts(region):
    return region // (PLANES * CORES), region // CORES % PLANES, region % CORES


def site(region):
    x, z, core = region_parts(region)
    place = (core * PAIR + z % PAIR) * COLUMNS + x
    return place * GROUPS + z // PAIR


def region_at(place, group):
    core, z, x = place // (PAIR * COLUMNS), place // COLUMNS % PAIR, place % COLUMNS
    return (x * PLANES + group * PAIR + z) * CORES + core


def weights_transposed(listed):
    neigh, regions = listed.shape
    owner = iota((regions, regions), 0)
    weight = (owner == iota((regions, regions), 1)).astype(F32)
    for place in range(neigh):
        weight = weight + TAPER ** (place + 1) * (listed[place : place + 1, :] == owner).astype(F32)
    return weight


def onehot(hit):
    return hit.astype(F32).astype(BF16)


def place_kernel(
    regions,
    capacity,
    owner_in,
    precision_in,
    obs_in,
    innovation_in,
    listed_in,
    rows_out,
    owner_ref,
    precision_ref,
    obs_ref,
    innovation_ref,
    listed_ref,
    rows_ref,
    arrivals,
    departures,
):
    copies = [
        pltpu.make_async_copy(source, target, arrivals.at[index])
        for index, (source, target) in enumerate(
            [
                (owner_in, owner_ref),
                (precision_in, precision_ref),
                (obs_in, obs_ref),
                (innovation_in, innovation_ref),
                (listed_in, listed_ref),
            ]
        )
    ]
    for copy in copies:
        copy.start()
    count = owner_ref.shape[1]
    blocks = count // LANES
    region_ids = iota((regions, LANES), 0)
    earlier = iota((LANES, LANES), 0) < iota((LANES, LANES), 1)
    counter = jnp.concatenate([onehot(earlier), jnp.ones((LANES, LANES), BF16)], axis=1)
    copies[0].wait()
    owners = owner_ref[...]
    named = [region_ids == owners[:, b * LANES : (b + 1) * LANES] for b in range(blocks)]
    ranks = dot(jnp.concatenate([onehot(hit) for hit in named], axis=0), counter)
    base = (site(region_ids) * capacity).astype(F32)
    pieces = []
    for b in range(blocks):
        part = ranks[b * regions : (b + 1) * regions]
        slot = jnp.where(named[b], part[:, :LANES] + base, 0.0)
        pieces.append(jnp.sum(slot, axis=0, keepdims=True))
        base = base + part[:, LANES:]
    slots = jnp.concatenate(pieces, axis=1).astype(jnp.int32)
    copies[1].wait()
    precision = precision_ref[...].astype(F32)
    scale = jnp.sqrt(precision)
    for copy in copies[2:]:
        copy.wait()
    obs = obs_ref[...]

    span = GROUPS * capacity
    at_once = 8
    sites = regions // GROUPS
    for start in range(0, sites, at_once):
        hit = slots == iota((at_once * span, count), 0) + start * span
        placed = dot(jnp.where(hit, scale, 0.0).astype(BF16), obs).astype(BF16)
        for k in range(at_once):
            rows_ref[start + k, :span, :] = placed[k * span : (k + 1) * span]
        if start == 0:
            part = (slice(0, at_once), slice(0, span))
            copy = pltpu.make_async_copy(rows_ref.at[part], rows_out.at[part], departures.at[0])
            copy.start()
            leaving = [copy]

    factor = precision * innovation_ref[...].astype(F32)
    hit = iota((regions, count), 0) == owners
    sums = split(dot(jnp.where(hit, factor, 0.0).astype(BF16), obs))
    half = obs[:, LANES:].astype(F32)
    squares = split(dot(jnp.where(hit, precision, 0.0).astype(BF16), (half * half).astype(BF16)))
    weight = split(weights_transposed(listed_ref[...]))
    row = iota((regions, sites * EXTRA), 1)
    place, item = row // EXTRA, row % EXTRA

    def chosen(group, valid):
        pick = onehot((iota((regions, sites * EXTRA), 0) == region_at(place, group)) & valid)
        return split(dot(weight[0], pick) + dot(weight[1], pick))

    over = ((0,), (0,))
    second = (item - GROUPS) * 2
    is_diag = (item >= GROUPS) & (item < GROUPS + GROUPS // 2)
    extra = dot3(chosen(item, item < GROUPS), sums, over)
    left = dot3(chosen(second, is_diag), squares, over)
    right = dot3(chosen(second + 1, is_diag), squares, over)
    extra = (extra + jnp.concatenate([left, right], axis=1)).astype(BF16)
    rows_ref[:, span:, :] = extra.reshape(sites, EXTRA, extra.shape[1])
    rest = [(slice(0, at_once), slice(span, span + EXTRA)), (slice(at_once, sites), slice(0, span + EXTRA))]
    for index, part in enumerate(rest):
        copy = pltpu.make_async_copy(rows_ref.at[part], rows_out.at[part], departures.at[index + 1])
        copy.start()
        leaving.append(copy)
    for copy in leaving:
        copy.wait()


def weight_kernel(listed_ref, high_ref, low_ref):
    size = high_ref.shape[0]
    weight = split(weights_transposed(listed_ref[...]))
    regions = listed_ref.shape[1]
    expand = onehot(iota((regions, size), 0) == iota((regions, size), 1) // SUBLANES)
    rows = split(dot(weight[0], expand) + dot(weight[1], expand))
    at = iota((regions, size), 1) // SUBLANES
    spread = onehot(iota((regions, size), 0) == region_at(at // GROUPS, at % GROUPS))
    over = ((0,), (0,))
    full = dot(rows[0], spread, over) + dot(rows[1], spread, over)
    same = iota((size, size), 0) % SUBLANES == iota((size, size), 1) % SUBLANES
    high, low = split(jnp.where(same, full, 0.0))
    high_ref[...] = high
    low_ref[...] = low


def covariance_kernel(capacity, rows_ref, message_ref, sums_ref):
    half = LANES
    members = rows_ref.shape[2]
    places = message_ref.shape[0]
    piece = members // places
    above = iota((half, half), 0) <= iota((half, half), 1)
    for group in range(GROUPS):
        rows = rows_ref[:, group * capacity : (group + 1) * capacity, :].reshape(-1, members)
        total = dot(rows, rows, ((0,), (0,)))
        corner = jnp.where(above, total[:half, :half], total[half:, half:])
        packed = jnp.concatenate([corner, total[:half, half:]], axis=0).astype(BF16)
        message_ref[:, group * piece : (group + 1) * piece, :] = packed.reshape(places, piece, LANES)
    span = GROUPS * capacity
    sums = jnp.sum(rows_ref[:, span : span + EXTRA, :].astype(F32), axis=0)
    for group in range(GROUPS):
        at, inner = GROUPS + group // 2, group % 2
        diagonal = sums[at : at + 1, inner * half : (inner + 1) * half]
        row = jnp.concatenate([sums[group : group + 1], diagonal], axis=1)
        sums_ref[group : group + 1, :] = row


def mix_kernel(message_ref, high_ref, low_ref, mixed_ref):
    places, rows, _ = message_ref.shape
    regions, piece, _ = mixed_ref.shape
    message = message_ref[...].reshape(regions, piece, LANES)
    parts = [
        message[:, at : at + SUBLANES, :].reshape(regions * SUBLANES, LANES) for at in range(0, piece, SUBLANES)
    ]
    wide = jnp.concatenate(parts, axis=1)
    mixed = (dot(high_ref[...], wide) + dot(low_ref[...], wide)).astype(BF16)
    for part in range(len(parts)):
        at = part * SUBLANES
        block = mixed[:, part * LANES : (part + 1) * LANES]
        mixed_ref[:, at : at + SUBLANES, :] = block.reshape(regions, SUBLANES, LANES)


def gather_kernel(pieces_ref, extra_ref, own_ref, sent_ref):
    regions, piece, _ = pieces_ref.shape
    size = regions // GROUPS * piece
    for place in range(regions // GROUPS):
        total = pieces_ref[region_at(place, 0)].astype(F32)
        for group in range(1, GROUPS):
            total = total + pieces_ref[region_at(place, group)].astype(F32)
        own_ref[place * piece : (place + 1) * piece, :] = total
        sent_ref[place * piece : (place + 1) * piece, :] = total.astype(BF16)
    extra = extra_ref[...]
    high = extra.astype(BF16).astype(F32)
    low = extra - high
    rows = [value[:, at : at + LANES] for value in (high, low) for at in range(0, 3 * LANES, LANES)]
    rows = jnp.concatenate(rows + [jnp.zeros((2, LANES), F32)], axis=0)
    own_ref[size:, :] = rows
    sent_ref[size:, :] = rows.astype(BF16)


def anomaly_kernel(ensemble_ref, average_ref, anomaly_ref):
    members, columns = ensemble_ref.shape
    for at in range(0, columns, WIDTH):
        block = ensemble_ref[:, at : at + WIDTH].astype(F32)
        average = jnp.sum(block, axis=0, keepdims=True) * (1.0 / members)
        average_ref[:, at : at + WIDTH] = average
        anomaly_ref[:, at : at + WIDTH] = (block - average).astype(BF16)


def transform_kernel(levels, level_ref, average_ref, anomaly_ref, own_ref, *refs):
    half = LANES
    size = 2 * half
    output_ref, block_ref, semaphores = refs[-3:]
    level = level_ref[0]
    everything = own_ref[...]
    for ahead in range(1, levels):
        source = lax.rem(level + (levels - ahead), levels)
        apart = jnp.abs(level - source)
        factor = jnp.where(apart == 1, DECAY, jnp.where(apart == 2, DECAY**2, DECAY**3))
        everything = everything + factor * refs[ahead - 1][...].astype(F32)
    extra = everything[size : size + 3] + everything[size + 3 : size + 6]
    tri = everything[:half]
    tri_t = tri.T
    cross = everything[half:size]
    row = iota((half, half), 0)
    col = iota((half, half), 1)
    first = jnp.where(row <= col, tri, tri_t)
    second = jnp.where(row > col, tri, tri_t)
    second = jnp.where(row == col, extra[2:3], second)
    matrix = jnp.concatenate(
        [jnp.concatenate([first, cross], axis=1), jnp.concatenate([cross.T, second], axis=1)], axis=0
    )
    same = iota((size, size), 0) == iota((size, size), 1)
    matrix = matrix + jnp.where(same, size - 1.0, 0.0)
    squares = jnp.sum(jnp.sum(matrix * matrix, axis=0, keepdims=True), axis=1, keepdims=True)
    norm_scale = 0.5 * jnp.sqrt(squares)
    diagonal = jnp.where(same, 1.5, 0.0)
    root_iter = matrix * (1.0 / norm_scale)
    correction = diagonal - 0.5 * root_iter
    inverse_iter = correction
    root_iter = dot3(split(root_iter), split(correction), halves=True)
    for newton_step in range(1, NSTEPS):
        inverse_split = split(inverse_iter)
        root_split = split(root_iter)
        correction = split(diagonal - 0.5 * dot3(inverse_split, root_split, halves=True))
        if newton_step < NSTEPS - 1:
            root_iter = dot3(root_split, correction)
        inverse_iter = dot3(correction, inverse_split)
    root = inverse_iter * (1.0 / jnp.sqrt(norm_scale))
    root_split = split(root)
    innovation = jnp.concatenate([extra[0:1], extra[1:2]], axis=1)
    innovation = jnp.broadcast_to(innovation, (SUBLANES, size))
    inner = dot3(split(innovation), root_split)
    mean_shift = dot3(split(inner), root_split)[0:1, :]
    transform = (math.sqrt(size - 1.0) * root + mean_shift).astype(BF16)
    copies = []
    for step, at in enumerate(range(0, anomaly_ref.shape[1], WIDTH)):
        span = slice(at, at + WIDTH)
        combined = dot(transform, anomaly_ref[:, span]) + average_ref[:, span]
        block_ref[:, span] = combined.astype(BF16)
        copy = pltpu.make_async_copy(
            block_ref.at[:, span], output_ref.at[:, span], semaphores.at[step]
        )
        copy.start()
        copies.append(copy)
    for copy in copies:
        copy.wait()


def call(
    kernel,
    shapes,
    *args,
    scratch=(),
    limit=VMEM_LIMIT,
    scalars=0,
    space=pltpu.VMEM,
    inputs=pltpu.VMEM,
):
    spaces = [pltpu.SMEM] * scalars + [inputs] * (len(args) - scalars)
    return pl.pallas_call(
        kernel,
        out_shape=shapes,
        in_specs=[pl.BlockSpec(memory_space=where) for where in spaces],
        out_specs=jax.tree.map(lambda _: pl.BlockSpec(memory_space=space), shapes),
        scratch_shapes=scratch,
        compiler_params=pltpu.CompilerParams(vmem_limit_bytes=limit),
    )(*args)


def body(ensemble, obs_anomaly, innovation, obs_precision, owner_region, neighbours):
    regions = lax.axis_size("region")
    levels = lax.axis_size("level")
    my_region = lax.axis_index("region")
    my_level = lax.axis_index("level")
    members = obs_anomaly.shape[2]
    local_obs = obs_anomaly.shape[1]
    capacity = 3 * local_obs // (2 * regions)
    places = regions // GROUPS
    owners = owner_region.reshape(1, local_obs)
    listed = neighbours.T
    shape = jax.ShapeDtypeStruct
    block = (places, GROUPS * capacity + EXTRA, members)
    rows = call(
        functools.partial(place_kernel, regions, capacity),
        shape(block, BF16),
        owners,
        obs_precision,
        obs_anomaly[0],
        innovation,
        listed,
        limit=FIRST_LIMIT,
        space=pl.ANY,
        inputs=pl.ANY,
        scratch=[
            pltpu.VMEM(owners.shape, jnp.int32),
            pltpu.VMEM(obs_precision.shape, BF16),
            pltpu.VMEM((local_obs, members), BF16),
            pltpu.VMEM(innovation.shape, BF16),
            pltpu.VMEM(listed.shape, jnp.int32),
            pltpu.VMEM(block, BF16),
            pltpu.SemaphoreType.DMA((5,)),
            pltpu.SemaphoreType.DMA((3,)),
        ],
    )
    near = [[region_at(place, group) for place in range(places)] for group in range(GROUPS)]
    routed = lax.all_to_all(rows, "region", 0, 0, tiled=True, axis_index_groups=near)
    piece = members // places
    high, low = call(
        weight_kernel, (shape((regions * SUBLANES, regions * SUBLANES), BF16),) * 2, listed
    )
    message, parts = call(
        functools.partial(covariance_kernel, capacity),
        (shape((places, GROUPS * piece, LANES), BF16), shape((GROUPS, members + LANES), F32)),
        routed,
    )
    message = lax.all_to_all(message, "region", 0, 0, tiled=True, axis_index_groups=near)
    mixed = call(mix_kernel, shape((regions, piece, LANES), BF16), message, high, low)
    mixed, parts = lax.optimization_barrier((mixed, parts))
    pieces = lax.all_to_all(mixed, "region", 0, 0, tiled=True)

    my_group = my_region // CORES % PLANES // PAIR
    part = lax.dynamic_slice_in_dim(parts, my_group, 1, 0)
    for ahead in range(1, GROUPS):
        sent = lax.dynamic_slice_in_dim(parts, (my_group + ahead) % GROUPS, 1, 0)
        pairs = []
        for region in range(regions):
            x, z, core = region_parts(region)
            pairs.append((region, (x * PLANES + (z + PAIR * ahead) % PLANES) * CORES + core))
        part = part + lax.ppermute(sent, "region", pairs)

    height = members + SUBLANES
    own, sent = call(
        gather_kernel, (shape((height, LANES), F32), shape((height, LANES), BF16)), pieces, part
    )
    arrived = [
        lax.ppermute(sent, "level", [(o, (o + ahead) % levels) for o in range(levels)])
        for ahead in range(1, levels)
    ]
    columns = ensemble.shape[2]
    average, anomaly = call(
        anomaly_kernel, (shape((1, columns), F32), shape((members, columns), BF16)), ensemble[0]
    )
    analysis = call(
        functools.partial(transform_kernel, levels),
        shape((members, columns), BF16),
        my_level.astype(jnp.int32).reshape(1),
        average,
        anomaly,
        own,
        *arrived,
        scalars=1,
        space=pl.ANY,
        scratch=[
            pltpu.VMEM((members, columns), BF16),
            pltpu.SemaphoreType.DMA((columns // WIDTH,)),
        ],
    )
    return analysis[None]


def solution(mesh):
    return jax.shard_map(
        body,
        mesh=mesh,
        in_specs=(
            P("level", None, "region"),
            P("level", "region", None),
            P("level", "region"),
            P("level", "region"),
            P("level", "region", None),
            P(),
        ),
        out_specs=P("level", None, "region"),
        check_vma=False,
    )
```

```python
import functools
import math

import jax
import jax.numpy as jnp
from jax import lax
from jax.experimental import pallas as pl
from jax.experimental.pallas import tpu as pltpu
from jax.sharding import PartitionSpec as P


NSTEPS = 4
TAPER = 0.6
DECAY = 0.5
LANES, SUBLANES = 128, 8
COLUMNS, PLANES, CORES = 4, 8, 2
PAIR = 2
GROUPS = PLANES // PAIR
WIDTH = 512
EXTRA = 16
VMEM_LIMIT = 16 << 20
FIRST_LIMIT = 62 << 20
BF16 = jnp.bfloat16
F32 = jnp.float32


def iota(shape, dim):
    return lax.broadcasted_iota(jnp.int32, shape, dim)


def dot(left, right, dims=((1,), (0,))):
    return lax.dot_general(left, right, (dims, ((), ())), preferred_element_type=F32)


def split(value):
    high = value.astype(BF16)
    return high, (value - high.astype(F32)).astype(BF16)


def dot3(left, right, dims=((1,), (0,)), halves=False):
    lh, ll = left
    rh, rl = right
    if dims != ((1,), (0,)):
        return dot(lh, rh, dims) + (dot(lh, rl, dims) + dot(ll, rh, dims))
    left = jnp.concatenate([lh, lh, ll], axis=1)
    right = jnp.concatenate([rh, rl, rh], axis=0)
    half = left.shape[0] // 2
    if halves and half >= LANES:
        return jnp.concatenate([dot(left[:half], right), dot(left[half:], right)], axis=0)
    return dot(left, right)


def region_parts(region):
    return region // (PLANES * CORES), region // CORES % PLANES, region % CORES


def site(region):
    x, z, core = region_parts(region)
    place = (core * PAIR + z % PAIR) * COLUMNS + x
    return place * GROUPS + z // PAIR


def region_at(place, group):
    core, z, x = place // (PAIR * COLUMNS), place // COLUMNS % PAIR, place % COLUMNS
    return (x * PLANES + group * PAIR + z) * CORES + core


def weights_transposed(listed):
    neigh, regions = listed.shape
    owner = iota((regions, regions), 0)
    weight = (owner == iota((regions, regions), 1)).astype(F32)
    for place in range(neigh):
        weight = weight + TAPER ** (place + 1) * (listed[place : place + 1, :] == owner).astype(F32)
    return weight


def onehot(hit):
    return hit.astype(F32).astype(BF16)


def place_kernel(
    regions,
    capacity,
    owner_in,
    precision_in,
    obs_in,
    rows_out,
    owner_ref,
    precision_ref,
    obs_ref,
    rows_ref,
    arrivals,
    departures,
):
    copies = [
        pltpu.make_async_copy(source, target, arrivals.at[index])
        for index, (source, target) in enumerate(
            [(owner_in, owner_ref), (precision_in, precision_ref), (obs_in, obs_ref)]
        )
    ]
    for copy in copies:
        copy.start()
    count = owner_ref.shape[1]
    blocks = count // LANES
    region_ids = iota((regions, LANES), 0)
    earlier = iota((LANES, LANES), 0) < iota((LANES, LANES), 1)
    counter = jnp.concatenate([onehot(earlier), jnp.ones((LANES, LANES), BF16)], axis=1)
    copies[0].wait()
    owners = owner_ref[...]
    named = [region_ids == owners[:, b * LANES : (b + 1) * LANES] for b in range(blocks)]
    ranks = dot(jnp.concatenate([onehot(hit) for hit in named], axis=0), counter)
    base = (site(region_ids) * capacity).astype(F32)
    pieces = []
    for b in range(blocks):
        part = ranks[b * regions : (b + 1) * regions]
        slot = jnp.where(named[b], part[:, :LANES] + base, 0.0)
        pieces.append(jnp.sum(slot, axis=0, keepdims=True))
        base = base + part[:, LANES:]
    slots = jnp.concatenate(pieces, axis=1).astype(jnp.int32)
    copies[1].wait()
    precision = precision_ref[...].astype(F32)
    scale = jnp.sqrt(precision)
    copies[2].wait()
    obs = obs_ref[...]

    span = GROUPS * capacity
    at_once = 8
    sites = regions // GROUPS
    for start in range(0, sites, at_once):
        hit = slots == iota((at_once * span, count), 0) + start * span
        placed = dot(jnp.where(hit, scale, 0.0).astype(BF16), obs).astype(BF16)
        for k in range(at_once):
            rows_ref[start + k] = placed[k * span : (k + 1) * span]
        if start == 0:
            part = slice(0, at_once)
            copy = pltpu.make_async_copy(rows_ref.at[part], rows_out.at[part], departures.at[0])
            copy.start()
            leaving = [copy]

    part = slice(at_once, sites)
    copy = pltpu.make_async_copy(rows_ref.at[part], rows_out.at[part], departures.at[1])
    copy.start()
    leaving.append(copy)
    for copy in leaving:
        copy.wait()


def sums_kernel(owner_ref, precision_ref, innovation_ref, obs_ref, listed_ref, sums_ref):
    count = owner_ref.shape[1]
    regions = listed_ref.shape[1]
    places, lines, _ = sums_ref.shape
    obs = obs_ref[...]
    precision = precision_ref[...].astype(F32)
    factor = precision * innovation_ref[...].astype(F32)
    hit = iota((regions, count), 0) == owner_ref[...]
    sums = dot(jnp.where(hit, factor, 0.0).astype(BF16), obs)
    half = obs[:, LANES:].astype(F32)
    squares = dot(jnp.where(hit, precision, 0.0).astype(BF16), (half * half).astype(BF16))
    weight = split(weights_transposed(listed_ref[...]))
    row = iota((regions, places * lines), 1)
    item = row % lines
    pick = iota((regions, places * lines), 0) == region_at(row // lines, item // 3)
    pick = onehot(pick & (item < 3 * GROUPS))
    chosen = split(dot(weight[0], pick) + dot(weight[1], pick))
    over = ((0,), (0,))
    parts = [dot3(chosen, split(value), over) for value in (sums[:, :LANES], sums[:, LANES:], squares)]
    kind = iota((places * lines, LANES), 0) % lines % 3
    mixed = jnp.where(kind == 0, parts[0], jnp.where(kind == 1, parts[1], parts[2]))
    sums_ref[...] = mixed.astype(BF16).reshape(places, lines, LANES)


def weight_kernel(listed_ref, high_ref, low_ref):
    size = high_ref.shape[0]
    weight = split(weights_transposed(listed_ref[...]))
    regions = listed_ref.shape[1]
    expand = onehot(iota((regions, size), 0) == iota((regions, size), 1) // SUBLANES)
    rows = split(dot(weight[0], expand) + dot(weight[1], expand))
    at = iota((regions, size), 1) // SUBLANES
    spread = onehot(iota((regions, size), 0) == region_at(at // GROUPS, at % GROUPS))
    over = ((0,), (0,))
    full = dot(rows[0], spread, over) + dot(rows[1], spread, over)
    same = iota((size, size), 0) % SUBLANES == iota((size, size), 1) % SUBLANES
    high, low = split(jnp.where(same, full, 0.0))
    high_ref[...] = high
    low_ref[...] = low


def covariance_kernel(capacity, rows_ref, sums_ref, message_ref):
    half = LANES
    members = rows_ref.shape[2]
    places = message_ref.shape[0]
    piece = members // places
    above = iota((half, half), 0) <= iota((half, half), 1)
    for group in range(GROUPS):
        rows = rows_ref[:, group * capacity : (group + 1) * capacity, :].reshape(-1, members)
        total = dot(rows, rows, ((0,), (0,)))
        corner = jnp.where(above, total[:half, :half], total[half:, half:])
        packed = jnp.concatenate([corner, total[:half, half:]], axis=0).astype(BF16)
        message_ref[:, group * piece : (group + 1) * piece, :] = packed.reshape(places, piece, LANES)
    message_ref[:, GROUPS * piece :, :] = sums_ref[...]


def mix_kernel(message_ref, high_ref, low_ref, mixed_ref, sums_ref):
    regions, piece, _ = mixed_ref.shape
    span = GROUPS * piece
    message = message_ref[:, :span, :].reshape(regions, piece, LANES)
    sums = jnp.sum(message_ref[:, span:, :].astype(F32), axis=0)
    for group in range(GROUPS):
        row = [sums[3 * group + part : 3 * group + part + 1] for part in range(3)]
        sums_ref[group : group + 1, :] = jnp.concatenate(row, axis=1)
    parts = [
        message[:, at : at + SUBLANES, :].reshape(regions * SUBLANES, LANES) for at in range(0, piece, SUBLANES)
    ]
    wide = jnp.concatenate(parts, axis=1)
    mixed = (dot(high_ref[...], wide) + dot(low_ref[...], wide)).astype(BF16)
    for part in range(len(parts)):
        at = part * SUBLANES
        block = mixed[:, part * LANES : (part + 1) * LANES]
        mixed_ref[:, at : at + SUBLANES, :] = block.reshape(regions, SUBLANES, LANES)


def gather_kernel(pieces_ref, extra_ref, own_ref, sent_ref):
    regions, piece, _ = pieces_ref.shape
    size = regions // GROUPS * piece
    for place in range(regions // GROUPS):
        total = pieces_ref[region_at(place, 0)].astype(F32)
        for group in range(1, GROUPS):
            total = total + pieces_ref[region_at(place, group)].astype(F32)
        own_ref[place * piece : (place + 1) * piece, :] = total
        sent_ref[place * piece : (place + 1) * piece, :] = total.astype(BF16)
    extra = extra_ref[...]
    high = extra.astype(BF16).astype(F32)
    low = extra - high
    rows = [value[:, at : at + LANES] for value in (high, low) for at in range(0, 3 * LANES, LANES)]
    rows = jnp.concatenate(rows + [jnp.zeros((2, LANES), F32)], axis=0)
    own_ref[size:, :] = rows
    sent_ref[size:, :] = rows.astype(BF16)


def anomaly_kernel(ensemble_ref, average_ref, anomaly_ref):
    members, columns = ensemble_ref.shape
    for at in range(0, columns, WIDTH):
        block = ensemble_ref[:, at : at + WIDTH].astype(F32)
        average = jnp.sum(block, axis=0, keepdims=True) * (1.0 / members)
        average_ref[:, at : at + WIDTH] = average
        anomaly_ref[:, at : at + WIDTH] = (block - average).astype(BF16)


def transform_kernel(levels, level_ref, average_ref, anomaly_ref, own_ref, *refs):
    half = LANES
    size = 2 * half
    output_ref, block_ref, semaphores = refs[-3:]
    level = level_ref[0]
    everything = own_ref[...]
    for ahead in range(1, levels):
        source = lax.rem(level + (levels - ahead), levels)
        apart = jnp.abs(level - source)
        factor = jnp.where(apart == 1, DECAY, jnp.where(apart == 2, DECAY**2, DECAY**3))
        everything = everything + factor * refs[ahead - 1][...].astype(F32)
    extra = everything[size : size + 3] + everything[size + 3 : size + 6]
    tri = everything[:half]
    tri_t = tri.T
    cross = everything[half:size]
    row = iota((half, half), 0)
    col = iota((half, half), 1)
    first = jnp.where(row <= col, tri, tri_t)
    second = jnp.where(row > col, tri, tri_t)
    second = jnp.where(row == col, extra[2:3], second)
    matrix = jnp.concatenate(
        [jnp.concatenate([first, cross], axis=1), jnp.concatenate([cross.T, second], axis=1)], axis=0
    )
    same = iota((size, size), 0) == iota((size, size), 1)
    matrix = matrix + jnp.where(same, size - 1.0, 0.0)
    squares = jnp.sum(jnp.sum(matrix * matrix, axis=0, keepdims=True), axis=1, keepdims=True)
    norm_scale = 0.5 * jnp.sqrt(squares)
    diagonal = jnp.where(same, 1.5, 0.0)
    root_iter = matrix * (1.0 / norm_scale)
    correction = diagonal - 0.5 * root_iter
    inverse_iter = correction
    root_iter = dot3(split(root_iter), split(correction), halves=True)
    for newton_step in range(1, NSTEPS):
        inverse_split = split(inverse_iter)
        root_split = split(root_iter)
        correction = split(diagonal - 0.5 * dot3(inverse_split, root_split, halves=True))
        if newton_step < NSTEPS - 1:
            root_iter = dot3(root_split, correction)
        inverse_iter = dot3(correction, inverse_split)
    root = inverse_iter * (1.0 / jnp.sqrt(norm_scale))
    innovation = jnp.concatenate([extra[0:1], extra[1:2]], axis=1)
    inner = jnp.sum(root * innovation, axis=1, keepdims=True)
    mean_shift = jnp.sum(inner * root, axis=0, keepdims=True)
    transform = (math.sqrt(size - 1.0) * root + mean_shift).astype(BF16)
    copies = []
    for step, at in enumerate(range(0, anomaly_ref.shape[1], WIDTH)):
        span = slice(at, at + WIDTH)
        combined = dot(transform, anomaly_ref[:, span]) + average_ref[:, span]
        block_ref[:, span] = combined.astype(BF16)
        copy = pltpu.make_async_copy(
            block_ref.at[:, span], output_ref.at[:, span], semaphores.at[step]
        )
        copy.start()
        copies.append(copy)
    for copy in copies:
        copy.wait()


def call(
    kernel,
    shapes,
    *args,
    scratch=(),
    limit=VMEM_LIMIT,
    scalars=0,
    space=pltpu.VMEM,
    inputs=pltpu.VMEM,
):
    spaces = [pltpu.SMEM] * scalars + [inputs] * (len(args) - scalars)
    return pl.pallas_call(
        kernel,
        out_shape=shapes,
        in_specs=[pl.BlockSpec(memory_space=where) for where in spaces],
        out_specs=jax.tree.map(lambda _: pl.BlockSpec(memory_space=space), shapes),
        scratch_shapes=scratch,
        compiler_params=pltpu.CompilerParams(vmem_limit_bytes=limit),
    )(*args)


def step(ensemble, obs_anomaly, innovation, obs_precision, owner_region, neighbours):
    regions = lax.axis_size("region")
    levels = lax.axis_size("level")
    my_region = lax.axis_index("region")
    my_level = lax.axis_index("level")
    members = obs_anomaly.shape[2]
    local_obs = obs_anomaly.shape[1]
    capacity = 3 * local_obs // (2 * regions)
    places = regions // GROUPS
    owners = owner_region.reshape(1, local_obs)
    listed = neighbours.T
    shape = jax.ShapeDtypeStruct
    block = (places, GROUPS * capacity, members)
    rows = call(
        functools.partial(place_kernel, regions, capacity),
        shape(block, BF16),
        owners,
        obs_precision,
        obs_anomaly[0],
        limit=FIRST_LIMIT,
        space=pl.ANY,
        inputs=pl.ANY,
        scratch=[
            pltpu.VMEM(owners.shape, jnp.int32),
            pltpu.VMEM(obs_precision.shape, BF16),
            pltpu.VMEM((local_obs, members), BF16),
            pltpu.VMEM(block, BF16),
            pltpu.SemaphoreType.DMA((3,)),
            pltpu.SemaphoreType.DMA((2,)),
        ],
    )
    near = [[region_at(place, group) for place in range(places)] for group in range(GROUPS)]
    routed = lax.all_to_all(rows, "region", 0, 0, tiled=True, axis_index_groups=near)
    piece = members // places
    high, low = call(
        weight_kernel, (shape((regions * SUBLANES, regions * SUBLANES), BF16),) * 2, listed
    )
    sums = call(
        sums_kernel,
        shape((places, EXTRA, LANES), BF16),
        owners,
        obs_precision,
        innovation,
        obs_anomaly[0],
        listed,
    )
    message = call(
        functools.partial(covariance_kernel, capacity),
        shape((places, GROUPS * piece + EXTRA, LANES), BF16),
        routed,
        sums,
    )
    message = lax.all_to_all(message, "region", 0, 0, tiled=True, axis_index_groups=near)
    mixed, parts = call(
        mix_kernel,
        (shape((regions, piece, LANES), BF16), shape((GROUPS, members + LANES), F32)),
        message,
        high,
        low,
    )
    pieces = lax.all_to_all(mixed, "region", 0, 0, tiled=True)

    my_group = my_region // CORES % PLANES // PAIR
    part = lax.dynamic_slice_in_dim(parts, my_group, 1, 0)
    for ahead in range(1, GROUPS):
        sent = lax.dynamic_slice_in_dim(parts, (my_group + ahead) % GROUPS, 1, 0)
        pairs = []
        for region in range(regions):
            x, z, core = region_parts(region)
            pairs.append((region, (x * PLANES + (z + PAIR * ahead) % PLANES) * CORES + core))
        part = part + lax.ppermute(sent, "region", pairs)

    height = members + SUBLANES
    own, sent = call(
        gather_kernel, (shape((height, LANES), F32), shape((height, LANES), BF16)), pieces, part
    )
    arrived = [
        lax.ppermute(sent, "level", [(o, (o + ahead) % levels) for o in range(levels)])
        for ahead in range(1, levels)
    ]
    columns = ensemble.shape[2]
    average, anomaly = call(
        anomaly_kernel,
        (shape((1, columns), F32), shape((members, columns), BF16)),
        ensemble[0],
        limit=FIRST_LIMIT,
    )
    analysis = call(
        functools.partial(transform_kernel, levels),
        shape((members, columns), BF16),
        my_level.astype(jnp.int32).reshape(1),
        average,
        anomaly,
        own,
        *arrived,
        scalars=1,
        space=pl.ANY,
        scratch=[
            pltpu.VMEM((members, columns), BF16),
            pltpu.SemaphoreType.DMA((columns // WIDTH,)),
        ],
    )
    return analysis[None]


def solution(mesh):
    return jax.shard_map(
        step,
        mesh=mesh,
        in_specs=(
            P("level", None, "region"),
            P("level", "region", None),
            P("level", "region"),
            P("level", "region"),
            P("level", "region", None),
            P(),
        ),
        out_specs=P("level", None, "region"),
        check_vma=False,
    )
```

```python
import functools
import math

import jax
import jax.numpy as jnp
from jax import lax
from jax.experimental import pallas as pl
from jax.experimental.pallas import tpu as pltpu
from jax.sharding import PartitionSpec as P


NSTEPS = 4
TAPER = 0.6
DECAY = 0.5
LANES, SUBLANES = 128, 8
COLUMNS, PLANES, CORES = 4, 8, 2
PAIR = 2
GROUPS = PLANES // PAIR
WIDTH = 512
EXTRA = 16
VMEM_LIMIT = 16 << 20
FIRST_LIMIT = 62 << 20
BF16 = jnp.bfloat16
F32 = jnp.float32


def iota(shape, dim):
    return lax.broadcasted_iota(jnp.int32, shape, dim)


def dot(left, right, dims=((1,), (0,))):
    return lax.dot_general(left, right, (dims, ((), ())), preferred_element_type=F32)


def split(value):
    high = value.astype(BF16)
    return high, (value - high.astype(F32)).astype(BF16)


def dot3(left, right, dims=((1,), (0,)), halves=False):
    lh, ll = left
    rh, rl = right
    if dims != ((1,), (0,)):
        return dot(lh, rh, dims) + (dot(lh, rl, dims) + dot(ll, rh, dims))
    left = jnp.concatenate([lh, lh, ll], axis=1)
    right = jnp.concatenate([rh, rl, rh], axis=0)
    half = left.shape[0] // 2
    if halves and half >= LANES:
        return jnp.concatenate([dot(left[:half], right), dot(left[half:], right)], axis=0)
    return dot(left, right)


def region_parts(region):
    return region // (PLANES * CORES), region // CORES % PLANES, region % CORES


def site(region):
    x, z, core = region_parts(region)
    place = (core * PAIR + z % PAIR) * COLUMNS + x
    return place * GROUPS + z // PAIR


def region_at(place, group):
    core, z, x = place // (PAIR * COLUMNS), place // COLUMNS % PAIR, place % COLUMNS
    return (x * PLANES + group * PAIR + z) * CORES + core


def weights_transposed(listed):
    neigh, regions = listed.shape
    owner = iota((regions, regions), 0)
    weight = (owner == iota((regions, regions), 1)).astype(F32)
    for place in range(neigh):
        weight = weight + TAPER ** (place + 1) * (listed[place : place + 1, :] == owner).astype(F32)
    return weight


def onehot(hit):
    return hit.astype(F32).astype(BF16)


def place_kernel(
    regions,
    capacity,
    owner_in,
    precision_in,
    obs_in,
    rows_out,
    owner_ref,
    precision_ref,
    obs_ref,
    rows_ref,
    arrivals,
    departures,
):
    copies = [
        pltpu.make_async_copy(source, target, arrivals.at[index])
        for index, (source, target) in enumerate(
            [(owner_in, owner_ref), (precision_in, precision_ref), (obs_in, obs_ref)]
        )
    ]
    for copy in copies:
        copy.start()
    count = owner_ref.shape[1]
    blocks = count // LANES
    region_ids = iota((regions, LANES), 0)
    earlier = iota((LANES, LANES), 0) < iota((LANES, LANES), 1)
    counter = jnp.concatenate([onehot(earlier), jnp.ones((LANES, LANES), BF16)], axis=1)
    copies[0].wait()
    owners = owner_ref[...]
    named = [region_ids == owners[:, b * LANES : (b + 1) * LANES] for b in range(blocks)]
    ranks = dot(jnp.concatenate([onehot(hit) for hit in named], axis=0), counter)
    base = (site(region_ids) * capacity).astype(F32)
    pieces = []
    for b in range(blocks):
        part = ranks[b * regions : (b + 1) * regions]
        slot = jnp.where(named[b], part[:, :LANES] + base, 0.0)
        pieces.append(jnp.sum(slot, axis=0, keepdims=True))
        base = base + part[:, LANES:]
    slots = jnp.concatenate(pieces, axis=1).astype(jnp.int32)
    copies[1].wait()
    precision = precision_ref[...].astype(F32)
    scale = jnp.sqrt(precision)
    copies[2].wait()
    obs = obs_ref[...]

    span = GROUPS * capacity
    at_once = 4
    leaving = []
    sites = regions // GROUPS
    for start in range(0, sites, at_once):
        hit = slots == iota((at_once * span, count), 0) + start * span
        placed = dot(jnp.where(hit, scale, 0.0).astype(BF16), obs).astype(BF16)
        for k in range(at_once):
            rows_ref[start + k] = placed[k * span : (k + 1) * span]
        part = slice(start, start + at_once)
        copy = pltpu.make_async_copy(
            rows_ref.at[part], rows_out.at[part], departures.at[start // at_once]
        )
        copy.start()
        leaving.append(copy)
    for copy in leaving:
        copy.wait()


def sums_kernel(owner_ref, precision_ref, innovation_ref, obs_ref, listed_ref, sums_ref):
    count = owner_ref.shape[1]
    regions = listed_ref.shape[1]
    places, lines, _ = sums_ref.shape
    obs = obs_ref[...]
    precision = precision_ref[...].astype(F32)
    factor = precision * innovation_ref[...].astype(F32)
    hit = iota((regions, count), 0) == owner_ref[...]
    sums = dot(jnp.where(hit, factor, 0.0).astype(BF16), obs)
    half = obs[:, LANES:].astype(F32)
    squares = dot(jnp.where(hit, precision, 0.0).astype(BF16), (half * half).astype(BF16))
    weight = split(weights_transposed(listed_ref[...]))
    row = iota((regions, places * lines), 1)
    item = row % lines
    pick = iota((regions, places * lines), 0) == region_at(row // lines, item // 3)
    pick = onehot(pick & (item < 3 * GROUPS))
    chosen = split(dot(weight[0], pick) + dot(weight[1], pick))
    over = ((0,), (0,))
    parts = [dot3(chosen, split(value), over) for value in (sums[:, :LANES], sums[:, LANES:], squares)]
    kind = iota((places * lines, LANES), 0) % lines % 3
    mixed = jnp.where(kind == 0, parts[0], jnp.where(kind == 1, parts[1], parts[2]))
    sums_ref[...] = mixed.astype(BF16).reshape(places, lines, LANES)


def weight_kernel(listed_ref, high_ref, low_ref):
    size = high_ref.shape[0]
    weight = split(weights_transposed(listed_ref[...]))
    regions = listed_ref.shape[1]
    expand = onehot(iota((regions, size), 0) == iota((regions, size), 1) // SUBLANES)
    rows = split(dot(weight[0], expand) + dot(weight[1], expand))
    at = iota((regions, size), 1) // SUBLANES
    spread = onehot(iota((regions, size), 0) == region_at(at // GROUPS, at % GROUPS))
    over = ((0,), (0,))
    full = dot(rows[0], spread, over) + dot(rows[1], spread, over)
    same = iota((size, size), 0) % SUBLANES == iota((size, size), 1) % SUBLANES
    high, low = split(jnp.where(same, full, 0.0))
    high_ref[...] = high
    low_ref[...] = low


def covariance_kernel(capacity, rows_ref, sums_ref, message_ref):
    half = LANES
    members = rows_ref.shape[2]
    places = message_ref.shape[0]
    piece = members // places
    above = iota((half, half), 0) <= iota((half, half), 1)
    for group in range(GROUPS):
        rows = rows_ref[:, group * capacity : (group + 1) * capacity, :].reshape(-1, members)
        total = dot(rows, rows, ((0,), (0,)))
        corner = jnp.where(above, total[:half, :half], total[half:, half:])
        packed = jnp.concatenate([corner, total[:half, half:]], axis=0).astype(BF16)
        message_ref[:, group * piece : (group + 1) * piece, :] = packed.reshape(places, piece, LANES)
    message_ref[:, GROUPS * piece :, :] = sums_ref[...]


def mix_kernel(message_ref, high_ref, low_ref, mixed_ref, sums_ref):
    regions, piece, _ = mixed_ref.shape
    span = GROUPS * piece
    message = message_ref[:, :span, :].reshape(regions, piece, LANES)
    sums = jnp.sum(message_ref[:, span:, :].astype(F32), axis=0)
    for group in range(GROUPS):
        row = [sums[3 * group + part : 3 * group + part + 1] for part in range(3)]
        sums_ref[group : group + 1, :] = jnp.concatenate(row, axis=1)
    parts = [
        message[:, at : at + SUBLANES, :].reshape(regions * SUBLANES, LANES) for at in range(0, piece, SUBLANES)
    ]
    wide = jnp.concatenate(parts, axis=1)
    mixed = (dot(high_ref[...], wide) + dot(low_ref[...], wide)).astype(BF16)
    for part in range(len(parts)):
        at = part * SUBLANES
        block = mixed[:, part * LANES : (part + 1) * LANES]
        mixed_ref[:, at : at + SUBLANES, :] = block.reshape(regions, SUBLANES, LANES)


def gather_kernel(pieces_ref, extra_ref, own_ref, sent_ref):
    regions, piece, _ = pieces_ref.shape
    size = regions // GROUPS * piece
    for place in range(regions // GROUPS):
        total = pieces_ref[region_at(place, 0)].astype(F32)
        for group in range(1, GROUPS):
            total = total + pieces_ref[region_at(place, group)].astype(F32)
        own_ref[place * piece : (place + 1) * piece, :] = total
        sent_ref[place * piece : (place + 1) * piece, :] = total.astype(BF16)
    extra = extra_ref[...]
    high = extra.astype(BF16).astype(F32)
    low = extra - high
    rows = [value[:, at : at + LANES] for value in (high, low) for at in range(0, 3 * LANES, LANES)]
    rows = jnp.concatenate(rows + [jnp.zeros((2, LANES), F32)], axis=0)
    own_ref[size:, :] = rows
    sent_ref[size:, :] = rows.astype(BF16)


def anomaly_kernel(ensemble_ref, average_ref, anomaly_ref):
    members, columns = ensemble_ref.shape
    for at in range(0, columns, WIDTH):
        block = ensemble_ref[:, at : at + WIDTH].astype(F32)
        average = jnp.sum(block, axis=0, keepdims=True) * (1.0 / members)
        average_ref[:, at : at + WIDTH] = average
        anomaly_ref[:, at : at + WIDTH] = (block - average).astype(BF16)


def transform_kernel(levels, level_ref, average_ref, anomaly_ref, own_ref, *refs):
    half = LANES
    size = 2 * half
    output_ref, block_ref, semaphores = refs[-3:]
    level = level_ref[0]
    everything = own_ref[...]
    for ahead in range(1, levels):
        source = lax.rem(level + (levels - ahead), levels)
        apart = jnp.abs(level - source)
        factor = jnp.where(apart == 1, DECAY, jnp.where(apart == 2, DECAY**2, DECAY**3))
        everything = everything + factor * refs[ahead - 1][...].astype(F32)
    extra = everything[size : size + 3] + everything[size + 3 : size + 6]
    tri = everything[:half]
    tri_t = tri.T
    cross = everything[half:size]
    row = iota((half, half), 0)
    col = iota((half, half), 1)
    first = jnp.where(row <= col, tri, tri_t)
    second = jnp.where(row > col, tri, tri_t)
    second = jnp.where(row == col, extra[2:3], second)
    matrix = jnp.concatenate(
        [jnp.concatenate([first, cross], axis=1), jnp.concatenate([cross.T, second], axis=1)], axis=0
    )
    same = iota((size, size), 0) == iota((size, size), 1)
    matrix = matrix + jnp.where(same, size - 1.0, 0.0)
    squares = jnp.sum(jnp.sum(matrix * matrix, axis=0, keepdims=True), axis=1, keepdims=True)
    norm_scale = 0.5 * jnp.sqrt(squares)
    inverse_scale = 1.0 / norm_scale
    diagonal = jnp.where(same, 1.5, 0.0)
    first_split = split(matrix)
    second_power = dot3(first_split, first_split, halves=True)
    third_power = dot3(first_split, split(second_power), halves=True)
    product = matrix * inverse_scale
    inverse_iter = diagonal - 0.5 * product
    product = (
        2.25 * product
        - (1.5 * inverse_scale**2) * second_power
        + (0.25 * inverse_scale**3) * third_power
    )
    for newton_step in range(1, NSTEPS):
        factor = split(product)
        if newton_step < NSTEPS - 1:
            square = dot3(factor, factor)
            inverse_step = dot3(split(inverse_iter), factor)
            cube = dot3(factor, split(square), halves=True)
            product = 2.25 * product - 1.5 * square + 0.25 * cube
        else:
            inverse_step = dot3(split(inverse_iter), factor, halves=True)
        inverse_iter = 1.5 * inverse_iter - 0.5 * inverse_step
    root = inverse_iter * (1.0 / jnp.sqrt(norm_scale))
    innovation = jnp.concatenate([extra[0:1], extra[1:2]], axis=1)
    inner = jnp.sum(root * innovation, axis=1, keepdims=True)
    mean_shift = jnp.sum(inner * root, axis=0, keepdims=True)
    transform = (math.sqrt(size - 1.0) * root + mean_shift).astype(BF16)
    copies = []
    for step, at in enumerate(range(0, anomaly_ref.shape[1], WIDTH)):
        span = slice(at, at + WIDTH)
        combined = dot(transform, anomaly_ref[:, span]) + average_ref[:, span]
        block_ref[:, span] = combined.astype(BF16)
        copy = pltpu.make_async_copy(
            block_ref.at[:, span], output_ref.at[:, span], semaphores.at[step]
        )
        copy.start()
        copies.append(copy)
    for copy in copies:
        copy.wait()


def call(
    kernel,
    shapes,
    *args,
    scratch=(),
    limit=VMEM_LIMIT,
    scalars=0,
    space=pltpu.VMEM,
    inputs=pltpu.VMEM,
):
    spaces = [pltpu.SMEM] * scalars + [inputs] * (len(args) - scalars)
    return pl.pallas_call(
        kernel,
        out_shape=shapes,
        in_specs=[pl.BlockSpec(memory_space=where) for where in spaces],
        out_specs=jax.tree.map(lambda _: pl.BlockSpec(memory_space=space), shapes),
        scratch_shapes=scratch,
        compiler_params=pltpu.CompilerParams(vmem_limit_bytes=limit),
    )(*args)


def step(ensemble, obs_anomaly, innovation, obs_precision, owner_region, neighbours):
    regions = lax.axis_size("region")
    levels = lax.axis_size("level")
    my_region = lax.axis_index("region")
    my_level = lax.axis_index("level")
    members = obs_anomaly.shape[2]
    local_obs = obs_anomaly.shape[1]
    capacity = 3 * local_obs // (2 * regions)
    places = regions // GROUPS
    owners = owner_region.reshape(1, local_obs)
    listed = neighbours.T
    shape = jax.ShapeDtypeStruct
    block = (places, GROUPS * capacity, members)
    rows = call(
        functools.partial(place_kernel, regions, capacity),
        shape(block, BF16),
        owners,
        obs_precision,
        obs_anomaly[0],
        limit=FIRST_LIMIT,
        space=pl.ANY,
        inputs=pl.ANY,
        scratch=[
            pltpu.VMEM(owners.shape, jnp.int32),
            pltpu.VMEM(obs_precision.shape, BF16),
            pltpu.VMEM((local_obs, members), BF16),
            pltpu.VMEM(block, BF16),
            pltpu.SemaphoreType.DMA((3,)),
            pltpu.SemaphoreType.DMA((4,)),
        ],
    )
    near = [[region_at(place, group) for place in range(places)] for group in range(GROUPS)]
    routed = lax.all_to_all(rows, "region", 0, 0, tiled=True, axis_index_groups=near)
    piece = members // places
    high, low = call(
        weight_kernel, (shape((regions * SUBLANES, regions * SUBLANES), BF16),) * 2, listed
    )
    sums = call(
        sums_kernel,
        shape((places, EXTRA, LANES), BF16),
        owners,
        obs_precision,
        innovation,
        obs_anomaly[0],
        listed,
    )
    message = call(
        functools.partial(covariance_kernel, capacity),
        shape((places, GROUPS * piece + EXTRA, LANES), BF16),
        routed,
        sums,
    )
    message = lax.all_to_all(message, "region", 0, 0, tiled=True, axis_index_groups=near)
    mixed, parts = call(
        mix_kernel,
        (shape((regions, piece, LANES), BF16), shape((GROUPS, members + LANES), F32)),
        message,
        high,
        low,
    )
    pieces = lax.all_to_all(mixed, "region", 0, 0, tiled=True)

    my_group = my_region // CORES % PLANES // PAIR
    part = lax.dynamic_slice_in_dim(parts, my_group, 1, 0)
    for ahead in range(1, GROUPS):
        sent = lax.dynamic_slice_in_dim(parts, (my_group + ahead) % GROUPS, 1, 0)
        pairs = []
        for region in range(regions):
            x, z, core = region_parts(region)
            pairs.append((region, (x * PLANES + (z + PAIR * ahead) % PLANES) * CORES + core))
        arrived_part = lax.ppermute(sent, "region", pairs)
        part = part + arrived_part

    height = members + SUBLANES
    own, sent = call(
        gather_kernel, (shape((height, LANES), F32), shape((height, LANES), BF16)), pieces, part
    )
    arrived = []
    for ahead in range(1, levels):
        pairs = [(level, (level + ahead) % levels) for level in range(levels)]
        arrived.append(lax.ppermute(sent, "level", pairs))
    columns = ensemble.shape[2]
    average, anomaly = call(
        anomaly_kernel,
        (shape((1, columns), F32), shape((members, columns), BF16)),
        ensemble[0],
        limit=FIRST_LIMIT,
    )
    analysis = call(
        functools.partial(transform_kernel, levels),
        shape((members, columns), BF16),
        my_level.astype(jnp.int32).reshape(1),
        average,
        anomaly,
        own,
        *arrived,
        scalars=1,
        space=pl.ANY,
        scratch=[
            pltpu.VMEM((members, columns), BF16),
            pltpu.SemaphoreType.DMA((columns // WIDTH,)),
        ],
    )
    return analysis[None]


def solution(mesh):
    return jax.shard_map(
        step,
        mesh=mesh,
        in_specs=(
            P("level", None, "region"),
            P("level", "region", None),
            P("level", "region"),
            P("level", "region"),
            P("level", "region", None),
            P(),
        ),
        out_specs=P("level", None, "region"),
        check_vma=False,
    )
```

```python
import functools
import math

import jax
import jax.numpy as jnp
from jax import lax
from jax.experimental import pallas as pl
from jax.experimental.pallas import tpu as pltpu
from jax.sharding import PartitionSpec as P


NSTEPS = 4
TAPER = 0.6
DECAY = 0.5
LANES, SUBLANES = 128, 8
COLUMNS, PLANES, CORES = 4, 8, 2
PAIR = 2
GROUPS = PLANES // PAIR
WIDTH = 512
EXTRA = 8
VMEM_LIMIT = 16 << 20
FIRST_LIMIT = 62 << 20
BF16 = jnp.bfloat16
F32 = jnp.float32


def iota(shape, dim):
    return lax.broadcasted_iota(jnp.int32, shape, dim)


def dot(left, right, dims=((1,), (0,))):
    return lax.dot_general(left, right, (dims, ((), ())), preferred_element_type=F32)


def split(value):
    high = value.astype(BF16)
    return high, (value - high.astype(F32)).astype(BF16)


def dot3(left, right, dims=((1,), (0,)), halves=False):
    lh, ll = left
    rh, rl = right
    if dims != ((1,), (0,)):
        return dot(lh, rh, dims) + (dot(lh, rl, dims) + dot(ll, rh, dims))
    left = jnp.concatenate([lh, lh, ll], axis=1)
    right = jnp.concatenate([rh, rl, rh], axis=0)
    half = left.shape[0] // 2
    if halves and half >= LANES:
        return jnp.concatenate([dot(left[:half], right), dot(left[half:], right)], axis=0)
    return dot(left, right)


def region_parts(region):
    return region // (PLANES * CORES), region // CORES % PLANES, region % CORES


def site(region):
    x, z, core = region_parts(region)
    place = (core * PAIR + z % PAIR) * COLUMNS + x
    return place * GROUPS + z // PAIR


def region_at(place, group):
    core, z, x = place // (PAIR * COLUMNS), place // COLUMNS % PAIR, place % COLUMNS
    return (x * PLANES + group * PAIR + z) * CORES + core


def weights_transposed(listed):
    neigh, regions = listed.shape
    owner = iota((regions, regions), 0)
    weight = (owner == iota((regions, regions), 1)).astype(F32)
    for place in range(neigh):
        weight = weight + TAPER ** (place + 1) * (listed[place : place + 1, :] == owner).astype(F32)
    return weight


def onehot(hit):
    return hit.astype(F32).astype(BF16)


def place_kernel(
    regions,
    capacity,
    owner_in,
    precision_in,
    obs_in,
    rows_out,
    owner_ref,
    precision_ref,
    obs_ref,
    rows_ref,
    arrivals,
    departures,
):
    copies = [
        pltpu.make_async_copy(source, target, arrivals.at[index])
        for index, (source, target) in enumerate(
            [(owner_in, owner_ref), (precision_in, precision_ref), (obs_in, obs_ref)]
        )
    ]
    for copy in copies:
        copy.start()
    count = owner_ref.shape[1]
    blocks = count // LANES
    region_ids = iota((regions, LANES), 0)
    earlier = iota((LANES, LANES), 0) < iota((LANES, LANES), 1)
    counter = jnp.concatenate([onehot(earlier), jnp.ones((LANES, LANES), BF16)], axis=1)
    copies[0].wait()
    owners = owner_ref[...]
    named = [region_ids == owners[:, b * LANES : (b + 1) * LANES] for b in range(blocks)]
    ranks = dot(jnp.concatenate([onehot(hit) for hit in named], axis=0), counter)
    base = (site(region_ids) * capacity).astype(F32)
    pieces = []
    for b in range(blocks):
        part = ranks[b * regions : (b + 1) * regions]
        slot = jnp.where(named[b], part[:, :LANES] + base, 0.0)
        pieces.append(jnp.sum(slot, axis=0, keepdims=True))
        base = base + part[:, LANES:]
    slots = jnp.concatenate(pieces, axis=1).astype(jnp.int32)
    copies[1].wait()
    precision = precision_ref[...].astype(F32)
    scale = jnp.sqrt(precision)
    copies[2].wait()
    obs = obs_ref[...]

    span = GROUPS * capacity
    at_once = 4
    leaving = []
    sites = regions // GROUPS
    for start in range(0, sites, at_once):
        hit = slots == iota((at_once * span, count), 0) + start * span
        placed = dot(jnp.where(hit, scale, 0.0).astype(BF16), obs).astype(BF16)
        for k in range(at_once):
            rows_ref[start + k] = placed[k * span : (k + 1) * span]
        part = slice(start, start + at_once)
        copy = pltpu.make_async_copy(
            rows_ref.at[part], rows_out.at[part], departures.at[start // at_once]
        )
        copy.start()
        leaving.append(copy)
    for copy in leaving:
        copy.wait()


def sums_kernel(owner_ref, precision_ref, innovation_ref, obs_ref, listed_ref, sums_ref):
    count = owner_ref.shape[1]
    regions = listed_ref.shape[1]
    groups, lines, _ = sums_ref.shape
    obs = obs_ref[...]
    precision = precision_ref[...].astype(F32)
    factor = precision * innovation_ref[...].astype(F32)
    hit = iota((regions, count), 0) == owner_ref[...]
    sums = dot(jnp.where(hit, factor, 0.0).astype(BF16), obs)
    half = obs[:, LANES:].astype(F32)
    squares = dot(jnp.where(hit, precision, 0.0).astype(BF16), (half * half).astype(BF16))
    weight = split(weights_transposed(listed_ref[...]))
    row = iota((regions, groups * lines), 1)
    item = row % EXTRA
    region = region_at(row % lines // EXTRA, row // lines)
    pick = onehot((iota((regions, groups * lines), 0) == region) & (item < 3))
    chosen = split(dot(weight[0], pick) + dot(weight[1], pick))
    over = ((0,), (0,))
    parts = [dot3(chosen, split(value), over) for value in (sums[:, :LANES], sums[:, LANES:], squares)]
    kind = iota((groups * lines, LANES), 0) % EXTRA
    mixed = jnp.where(kind == 0, parts[0], jnp.where(kind == 1, parts[1], parts[2]))
    sums_ref[...] = mixed.astype(BF16).reshape(groups, lines, LANES)


def weight_kernel(listed_ref, high_ref, low_ref):
    size = high_ref.shape[0]
    weight = split(weights_transposed(listed_ref[...]))
    regions = listed_ref.shape[1]
    expand = onehot(iota((regions, size), 0) == iota((regions, size), 1) // SUBLANES)
    rows = split(dot(weight[0], expand) + dot(weight[1], expand))
    at = iota((regions, size), 1) // SUBLANES
    spread = onehot(iota((regions, size), 0) == region_at(at // GROUPS, at % GROUPS))
    over = ((0,), (0,))
    full = dot(rows[0], spread, over) + dot(rows[1], spread, over)
    same = iota((size, size), 0) % SUBLANES == iota((size, size), 1) % SUBLANES
    high, low = split(jnp.where(same, full, 0.0))
    high_ref[...] = high
    low_ref[...] = low


def covariance_kernel(capacity, rows_ref, sums_ref, message_out, message_ref, semaphores):
    half = LANES
    members = rows_ref.shape[2]
    places = message_ref.shape[0]
    piece = members // places
    above = iota((half, half), 0) <= iota((half, half), 1)
    for group in range(GROUPS):
        rows = rows_ref[:, group * capacity : (group + 1) * capacity, :].reshape(-1, members)
        total = dot(rows, rows, ((0,), (0,)))
        corner = jnp.where(above, total[:half, :half], total[half:, half:])
        packed = jnp.concatenate([corner, total[:half, half:]], axis=0).astype(BF16)
        message_ref[:, group * piece : (group + 1) * piece, :] = packed.reshape(places, piece, LANES)
        if group == GROUPS // 2 - 1:
            part = slice(0, (group + 1) * piece)
            first = pltpu.make_async_copy(
                message_ref.at[:, part], message_out.at[:, part], semaphores.at[0]
            )
            first.start()
    message_ref[:, GROUPS * piece :, :] = sums_ref[...].reshape(places, EXTRA, LANES)
    part = slice(GROUPS // 2 * piece, GROUPS * piece + EXTRA)
    second = pltpu.make_async_copy(
        message_ref.at[:, part], message_out.at[:, part], semaphores.at[1]
    )
    second.start()
    first.wait()
    second.wait()


def mix_kernel(message_ref, high_ref, low_ref, mixed_ref, sums_ref):
    regions, piece, _ = mixed_ref.shape
    span = GROUPS * piece
    message = message_ref[:, :span, :].reshape(regions, piece, LANES)
    sums = jnp.sum(message_ref[:, span:, :].astype(F32), axis=0)
    sums_ref[...] = jnp.concatenate([sums[part : part + 1] for part in range(3)], axis=1)
    parts = [
        message[:, at : at + SUBLANES, :].reshape(regions * SUBLANES, LANES) for at in range(0, piece, SUBLANES)
    ]
    wide = jnp.concatenate(parts, axis=1)
    mixed = (dot(high_ref[...], wide) + dot(low_ref[...], wide)).astype(BF16)
    for part in range(len(parts)):
        at = part * SUBLANES
        block = mixed[:, part * LANES : (part + 1) * LANES]
        mixed_ref[:, at : at + SUBLANES, :] = block.reshape(regions, SUBLANES, LANES)


def gather_kernel(pieces_ref, extra_ref, own_ref, sent_ref):
    regions, piece, _ = pieces_ref.shape
    size = regions // GROUPS * piece
    for place in range(regions // GROUPS):
        total = pieces_ref[region_at(place, 0)].astype(F32)
        for group in range(1, GROUPS):
            total = total + pieces_ref[region_at(place, group)].astype(F32)
        own_ref[place * piece : (place + 1) * piece, :] = total
        sent_ref[place * piece : (place + 1) * piece, :] = total.astype(BF16)
    extra = extra_ref[...]
    high = extra.astype(BF16).astype(F32)
    low = extra - high
    rows = [value[:, at : at + LANES] for value in (high, low) for at in range(0, 3 * LANES, LANES)]
    rows = jnp.concatenate(rows + [jnp.zeros((2, LANES), F32)], axis=0)
    own_ref[size:, :] = rows
    sent_ref[size:, :] = rows.astype(BF16)


def anomaly_kernel(ensemble_ref, average_ref, anomaly_ref):
    members, columns = ensemble_ref.shape
    for at in range(0, columns, WIDTH):
        block = ensemble_ref[:, at : at + WIDTH].astype(F32)
        average = jnp.sum(block, axis=0, keepdims=True) * (1.0 / members)
        average_ref[:, at : at + WIDTH] = average
        anomaly_ref[:, at : at + WIDTH] = (block - average).astype(BF16)


def transform_kernel(levels, level_ref, average_ref, anomaly_ref, own_ref, *refs):
    half = LANES
    size = 2 * half
    output_ref, block_ref, semaphores = refs[-3:]
    level = level_ref[0]
    everything = own_ref[...]
    for ahead in range(1, levels):
        source = lax.rem(level + (levels - ahead), levels)
        apart = jnp.abs(level - source)
        factor = jnp.where(apart == 1, DECAY, jnp.where(apart == 2, DECAY**2, DECAY**3))
        everything = everything + factor * refs[ahead - 1][...].astype(F32)
    extra = everything[size : size + 3] + everything[size + 3 : size + 6]
    tri = everything[:half]
    tri_t = tri.T
    cross = everything[half:size]
    row = iota((half, half), 0)
    col = iota((half, half), 1)
    first = jnp.where(row <= col, tri, tri_t)
    second = jnp.where(row > col, tri, tri_t)
    second = jnp.where(row == col, extra[2:3], second)
    matrix = jnp.concatenate(
        [jnp.concatenate([first, cross], axis=1), jnp.concatenate([cross.T, second], axis=1)], axis=0
    )
    same = iota((size, size), 0) == iota((size, size), 1)
    matrix = matrix + jnp.where(same, size - 1.0, 0.0)
    squares = jnp.sum(jnp.sum(matrix * matrix, axis=0, keepdims=True), axis=1, keepdims=True)
    norm_scale = 0.5 * jnp.sqrt(squares)
    inverse_scale = 1.0 / norm_scale
    diagonal = jnp.where(same, 1.5, 0.0)
    first_split = split(matrix)
    second_power = dot3(first_split, first_split, halves=True)
    third_power = dot3(first_split, split(second_power), halves=True)
    product = matrix * inverse_scale
    inverse_iter = diagonal - 0.5 * product
    product = (
        2.25 * product
        - (1.5 * inverse_scale**2) * second_power
        + (0.25 * inverse_scale**3) * third_power
    )
    for newton_step in range(1, NSTEPS):
        factor = split(product)
        if newton_step < NSTEPS - 1:
            square = dot3(factor, factor)
            inverse_step = dot3(split(inverse_iter), factor)
            cube = dot3(factor, split(square), halves=True)
            product = 2.25 * product - 1.5 * square + 0.25 * cube
        else:
            inverse_step = dot3(split(inverse_iter), factor, halves=True)
        inverse_iter = 1.5 * inverse_iter - 0.5 * inverse_step
    root = inverse_iter * (1.0 / jnp.sqrt(norm_scale))
    innovation = jnp.concatenate([extra[0:1], extra[1:2]], axis=1)
    inner = jnp.sum(root * innovation, axis=1, keepdims=True)
    mean_shift = jnp.sum(inner * root, axis=0, keepdims=True)
    transform = (math.sqrt(size - 1.0) * root + mean_shift).astype(BF16)
    copies = []
    for step, at in enumerate(range(0, anomaly_ref.shape[1], WIDTH)):
        span = slice(at, at + WIDTH)
        combined = dot(transform, anomaly_ref[:, span]) + average_ref[:, span]
        block_ref[:, span] = combined.astype(BF16)
        copy = pltpu.make_async_copy(
            block_ref.at[:, span], output_ref.at[:, span], semaphores.at[step]
        )
        copy.start()
        copies.append(copy)
    for copy in copies:
        copy.wait()


def call(
    kernel,
    shapes,
    *args,
    scratch=(),
    limit=VMEM_LIMIT,
    scalars=0,
    space=pltpu.VMEM,
    inputs=pltpu.VMEM,
):
    spaces = [pltpu.SMEM] * scalars + [inputs] * (len(args) - scalars)
    return pl.pallas_call(
        kernel,
        out_shape=shapes,
        in_specs=[pl.BlockSpec(memory_space=where) for where in spaces],
        out_specs=jax.tree.map(lambda _: pl.BlockSpec(memory_space=space), shapes),
        scratch_shapes=scratch,
        compiler_params=pltpu.CompilerParams(vmem_limit_bytes=limit),
    )(*args)


def step(ensemble, obs_anomaly, innovation, obs_precision, owner_region, neighbours):
    regions = lax.axis_size("region")
    levels = lax.axis_size("level")
    my_region = lax.axis_index("region")
    my_level = lax.axis_index("level")
    members = obs_anomaly.shape[2]
    local_obs = obs_anomaly.shape[1]
    capacity = 3 * local_obs // (2 * regions)
    places = regions // GROUPS
    owners = owner_region.reshape(1, local_obs)
    listed = neighbours.T
    shape = jax.ShapeDtypeStruct
    block = (places, GROUPS * capacity, members)
    rows = call(
        functools.partial(place_kernel, regions, capacity),
        shape(block, BF16),
        owners,
        obs_precision,
        obs_anomaly[0],
        limit=FIRST_LIMIT,
        space=pl.ANY,
        inputs=pl.ANY,
        scratch=[
            pltpu.VMEM(owners.shape, jnp.int32),
            pltpu.VMEM(obs_precision.shape, BF16),
            pltpu.VMEM((local_obs, members), BF16),
            pltpu.VMEM(block, BF16),
            pltpu.SemaphoreType.DMA((3,)),
            pltpu.SemaphoreType.DMA((4,)),
        ],
    )
    near = [[region_at(place, group) for place in range(places)] for group in range(GROUPS)]
    routed = lax.all_to_all(rows, "region", 0, 0, tiled=True, axis_index_groups=near)
    piece = members // places
    high, low = call(
        weight_kernel, (shape((regions * SUBLANES, regions * SUBLANES), BF16),) * 2, listed
    )
    sums = call(
        sums_kernel,
        shape((GROUPS, places * EXTRA, LANES), BF16),
        owners,
        obs_precision,
        innovation,
        obs_anomaly[0],
        listed,
    )
    my_group = my_region // CORES % PLANES // PAIR
    total = lax.dynamic_index_in_dim(sums, my_group, 0, keepdims=False).astype(F32)
    for ahead in range(1, GROUPS):
        sent = lax.dynamic_index_in_dim(sums, (my_group + ahead) % GROUPS, 0, keepdims=False)
        pairs = []
        for region in range(regions):
            x, z, core = region_parts(region)
            pairs.append((region, (x * PLANES + (z + PAIR * ahead) % PLANES) * CORES + core))
        arrived_part = lax.ppermute(sent, "region", pairs)
        total = total + arrived_part.astype(F32)
    total = total.astype(BF16)
    block = (places, GROUPS * piece + EXTRA, LANES)
    message = call(
        functools.partial(covariance_kernel, capacity),
        shape(block, BF16),
        routed,
        total,
        space=pltpu.HBM,
        scratch=[pltpu.VMEM(block, BF16), pltpu.SemaphoreType.DMA((2,))],
    )
    message = lax.all_to_all(message, "region", 0, 0, tiled=True, axis_index_groups=near)
    mixed, part = call(
        mix_kernel,
        (shape((regions, piece, LANES), BF16), shape((1, members + LANES), F32)),
        message,
        high,
        low,
    )
    pieces = lax.all_to_all(mixed, "region", 0, 0, tiled=True)

    height = members + SUBLANES
    own, sent = call(
        gather_kernel, (shape((height, LANES), F32), shape((height, LANES), BF16)), pieces, part
    )
    arrived = []
    for ahead in range(1, levels):
        pairs = [(level, (level + ahead) % levels) for level in range(levels)]
        arrived.append(lax.ppermute(sent, "level", pairs))
    columns = ensemble.shape[2]
    average, anomaly = call(
        anomaly_kernel,
        (shape((1, columns), F32), shape((members, columns), BF16)),
        ensemble[0],
        limit=FIRST_LIMIT,
    )
    analysis = call(
        functools.partial(transform_kernel, levels),
        shape((members, columns), BF16),
        my_level.astype(jnp.int32).reshape(1),
        average,
        anomaly,
        own,
        *arrived,
        scalars=1,
        space=pl.ANY,
        scratch=[
            pltpu.VMEM((members, columns), BF16),
            pltpu.SemaphoreType.DMA((columns // WIDTH,)),
        ],
    )
    return analysis[None]


def solution(mesh):
    return jax.shard_map(
        step,
        mesh=mesh,
        in_specs=(
            P("level", None, "region"),
            P("level", "region", None),
            P("level", "region"),
            P("level", "region"),
            P("level", "region", None),
            P(),
        ),
        out_specs=P("level", None, "region"),
        check_vma=False,
    )
```

```python
import functools
import math

import jax
import jax.numpy as jnp
from jax import lax
from jax.experimental import pallas as pl
from jax.experimental.pallas import tpu as pltpu
from jax.sharding import PartitionSpec as P


NSTEPS = 4
TAPER = 0.6
DECAY = 0.5
LANES, SUBLANES = 128, 8
COLUMNS, PLANES, CORES = 4, 8, 2
PAIR = 2
GROUPS = PLANES // PAIR
WIDTH = 512
ROWS = 3
EXTRA = 8
VMEM_LIMIT = 16 << 20
FIRST_LIMIT = 62 << 20
BF16 = jnp.bfloat16
F32 = jnp.float32


def iota(shape, dim):
    return lax.broadcasted_iota(jnp.int32, shape, dim)


def dot(left, right, dims=((1,), (0,))):
    return lax.dot_general(left, right, (dims, ((), ())), preferred_element_type=F32)


def split(value):
    high = value.astype(BF16)
    return high, (value - high.astype(F32)).astype(BF16)


def dot3(left, right, dims=((1,), (0,)), halves=False):
    lh, ll = left
    rh, rl = right
    if dims != ((1,), (0,)):
        return dot(lh, rh, dims) + (dot(lh, rl, dims) + dot(ll, rh, dims))
    left = jnp.concatenate([lh, lh, ll], axis=1)
    right = jnp.concatenate([rh, rl, rh], axis=0)
    half = left.shape[0] // 2
    if halves and half >= LANES:
        return jnp.concatenate([dot(left[:half], right), dot(left[half:], right)], axis=0)
    return dot(left, right)


def region_parts(region):
    return region // (PLANES * CORES), region // CORES % PLANES, region % CORES


def site(region):
    x, z, core = region_parts(region)
    place = (core * PAIR + z % PAIR) * COLUMNS + x
    return place * GROUPS + z // PAIR


def region_at(place, group):
    core, z, x = place // (PAIR * COLUMNS), place // COLUMNS % PAIR, place % COLUMNS
    return (x * PLANES + group * PAIR + z) * CORES + core


def weights_transposed(listed):
    neigh, regions = listed.shape
    owner = iota((regions, regions), 0)
    weight = (owner == iota((regions, regions), 1)).astype(F32)
    for place in range(neigh):
        weight = weight + TAPER ** (place + 1) * (listed[place : place + 1, :] == owner).astype(F32)
    return weight


def onehot(hit):
    return hit.astype(F32).astype(BF16)


def place_kernel(
    regions,
    capacity,
    owner_in,
    precision_in,
    obs_in,
    rows_out,
    owner_ref,
    precision_ref,
    obs_ref,
    rows_ref,
    arrivals,
    departures,
):
    copies = [
        pltpu.make_async_copy(source, target, arrivals.at[index])
        for index, (source, target) in enumerate(
            [(owner_in, owner_ref), (precision_in, precision_ref), (obs_in, obs_ref)]
        )
    ]
    for copy in copies:
        copy.start()
    count = owner_ref.shape[1]
    blocks = count // LANES
    region_ids = iota((regions, LANES), 0)
    earlier = iota((LANES, LANES), 0) < iota((LANES, LANES), 1)
    counter = jnp.concatenate([onehot(earlier), jnp.ones((LANES, LANES), BF16)], axis=1)
    copies[0].wait()
    owners = owner_ref[...]
    named = [region_ids == owners[:, b * LANES : (b + 1) * LANES] for b in range(blocks)]
    ranks = dot(jnp.concatenate([onehot(hit) for hit in named], axis=0), counter)
    base = (site(region_ids) * capacity).astype(F32)
    pieces = []
    for b in range(blocks):
        part = ranks[b * regions : (b + 1) * regions]
        slot = jnp.where(named[b], part[:, :LANES] + base, 0.0)
        pieces.append(jnp.sum(slot, axis=0, keepdims=True))
        base = base + part[:, LANES:]
    slots = jnp.concatenate(pieces, axis=1).astype(jnp.int32)
    copies[1].wait()
    precision = precision_ref[...].astype(F32)
    scale = jnp.sqrt(precision)
    copies[2].wait()
    obs = obs_ref[...]

    span = GROUPS * capacity
    at_once = 4
    leaving = []
    sites = regions // GROUPS
    for start in range(0, sites, at_once):
        hit = slots == iota((at_once * span, count), 0) + start * span
        placed = dot(jnp.where(hit, scale, 0.0).astype(BF16), obs).astype(BF16)
        for k in range(at_once):
            rows_ref[start + k] = placed[k * span : (k + 1) * span]
        part = slice(start, start + at_once)
        copy = pltpu.make_async_copy(
            rows_ref.at[part], rows_out.at[part], departures.at[start // at_once]
        )
        copy.start()
        leaving.append(copy)
    for copy in leaving:
        copy.wait()


def sums_kernel(owner_ref, precision_ref, innovation_ref, obs_ref, listed_ref, sums_ref):
    count = owner_ref.shape[1]
    regions = listed_ref.shape[1]
    groups, lines, _ = sums_ref.shape
    obs = obs_ref[...]
    precision = precision_ref[...].astype(F32)
    factor = precision * innovation_ref[...].astype(F32)
    hit = iota((regions, count), 0) == owner_ref[...]
    sums = dot(jnp.where(hit, factor, 0.0).astype(BF16), obs)
    half = obs[:, LANES:].astype(F32)
    squares = dot(jnp.where(hit, precision, 0.0).astype(BF16), (half * half).astype(BF16))
    weight = split(weights_transposed(listed_ref[...]))
    row = iota((regions, groups * lines), 1)
    region = region_at(row % lines // ROWS, row // lines)
    pick = onehot(iota((regions, groups * lines), 0) == region)
    chosen = split(dot(weight[0], pick) + dot(weight[1], pick))
    over = ((0,), (0,))
    parts = [dot3(chosen, split(value), over) for value in (sums[:, :LANES], sums[:, LANES:], squares)]
    kind = iota((groups * lines, LANES), 0) % ROWS
    mixed = jnp.where(kind == 0, parts[0], jnp.where(kind == 1, parts[1], parts[2]))
    sums_ref[...] = mixed.astype(BF16).reshape(groups, lines, LANES)


def weight_kernel(listed_ref, high_ref, low_ref):
    size = high_ref.shape[0]
    weight = split(weights_transposed(listed_ref[...]))
    regions = listed_ref.shape[1]
    expand = onehot(iota((regions, size), 0) == iota((regions, size), 1) // SUBLANES)
    rows = split(dot(weight[0], expand) + dot(weight[1], expand))
    at = iota((regions, size), 1) // SUBLANES
    spread = onehot(iota((regions, size), 0) == region_at(at // GROUPS, at % GROUPS))
    over = ((0,), (0,))
    full = dot(rows[0], spread, over) + dot(rows[1], spread, over)
    same = iota((size, size), 0) % SUBLANES == iota((size, size), 1) % SUBLANES
    high, low = split(jnp.where(same, full, 0.0))
    high_ref[...] = high
    low_ref[...] = low


def covariance_kernel(capacity, rows_ref, sums_ref, message_out, message_ref, semaphores):
    half = LANES
    members = rows_ref.shape[2]
    places = message_ref.shape[0]
    piece = members // places
    above = iota((half, half), 0) <= iota((half, half), 1)
    for group in range(GROUPS):
        rows = rows_ref[:, group * capacity : (group + 1) * capacity, :].reshape(-1, members)
        total = dot(rows, rows, ((0,), (0,)))
        corner = jnp.where(above, total[:half, :half], total[half:, half:])
        packed = jnp.concatenate([corner, total[:half, half:]], axis=0).astype(BF16)
        message_ref[:, group * piece : (group + 1) * piece, :] = packed.reshape(places, piece, LANES)
        if group == GROUPS // 2 - 1:
            part = slice(0, (group + 1) * piece)
            first = pltpu.make_async_copy(
                message_ref.at[:, part], message_out.at[:, part], semaphores.at[0]
            )
            first.start()
    wide = (places * EXTRA, 2 * places * ROWS)
    line = iota(wide, 0)
    item = line % EXTRA
    source = item // ROWS * (places * ROWS) + line // EXTRA * ROWS + item % ROWS
    spread = (item < 2 * ROWS) & (source == iota(wide, 1))
    sums = dot(onehot(spread), sums_ref[...]).astype(BF16)
    message_ref[:, GROUPS * piece :, :] = sums.reshape(places, EXTRA, LANES)
    part = slice(GROUPS // 2 * piece, GROUPS * piece + EXTRA)
    second = pltpu.make_async_copy(
        message_ref.at[:, part], message_out.at[:, part], semaphores.at[1]
    )
    second.start()
    first.wait()
    second.wait()


def mix_kernel(message_ref, high_ref, low_ref, mixed_ref, sums_ref):
    regions, piece, _ = mixed_ref.shape
    span = GROUPS * piece
    message = message_ref[:, :span, :].reshape(regions, piece, LANES)
    sums = jnp.sum(message_ref[:, span:, :].astype(F32), axis=0)
    for index in range(2):
        row = [sums[at : at + 1] for at in range(index * ROWS, (index + 1) * ROWS)]
        sums_ref[index : index + 1, :] = jnp.concatenate(row, axis=1)
    parts = [
        message[:, at : at + SUBLANES, :].reshape(regions * SUBLANES, LANES) for at in range(0, piece, SUBLANES)
    ]
    wide = jnp.concatenate(parts, axis=1)
    mixed = (dot(high_ref[...], wide) + dot(low_ref[...], wide)).astype(BF16)
    for part in range(len(parts)):
        at = part * SUBLANES
        block = mixed[:, part * LANES : (part + 1) * LANES]
        mixed_ref[:, at : at + SUBLANES, :] = block.reshape(regions, SUBLANES, LANES)


def gather_kernel(pieces_ref, extra_ref, own_ref, sent_ref):
    regions, piece, _ = pieces_ref.shape
    size = regions // GROUPS * piece
    for place in range(regions // GROUPS):
        total = pieces_ref[region_at(place, 0)].astype(F32)
        for group in range(1, GROUPS):
            total = total + pieces_ref[region_at(place, group)].astype(F32)
        own_ref[place * piece : (place + 1) * piece, :] = total
        sent_ref[place * piece : (place + 1) * piece, :] = total.astype(BF16)
    extra = extra_ref[...]
    high = extra.astype(BF16).astype(F32)
    low = extra - high
    rows = [value[:, at : at + LANES] for value in (high, low) for at in range(0, 3 * LANES, LANES)]
    rows = jnp.concatenate(rows + [jnp.zeros((2, LANES), F32)], axis=0)
    own_ref[size:, :] = rows
    sent_ref[size:, :] = rows.astype(BF16)


def anomaly_kernel(ensemble_ref, average_ref, anomaly_ref):
    members, columns = ensemble_ref.shape
    for at in range(0, columns, WIDTH):
        block = ensemble_ref[:, at : at + WIDTH].astype(F32)
        average = jnp.sum(block, axis=0, keepdims=True) * (1.0 / members)
        average_ref[:, at : at + WIDTH] = average
        anomaly_ref[:, at : at + WIDTH] = (block - average).astype(BF16)


def transform_kernel(levels, level_ref, average_ref, anomaly_ref, own_ref, *refs):
    half = LANES
    size = 2 * half
    output_ref, block_ref, semaphores = refs[-3:]
    level = level_ref[0]
    everything = own_ref[...]
    for ahead in range(1, levels):
        source = lax.rem(level + (levels - ahead), levels)
        apart = jnp.abs(level - source)
        factor = jnp.where(apart == 1, DECAY, jnp.where(apart == 2, DECAY**2, DECAY**3))
        everything = everything + factor * refs[ahead - 1][...].astype(F32)
    extra = everything[size : size + 3] + everything[size + 3 : size + 6]
    tri = everything[:half]
    tri_t = tri.T
    cross = everything[half:size]
    row = iota((half, half), 0)
    col = iota((half, half), 1)
    first = jnp.where(row <= col, tri, tri_t)
    second = jnp.where(row > col, tri, tri_t)
    second = jnp.where(row == col, extra[2:3], second)
    matrix = jnp.concatenate(
        [jnp.concatenate([first, cross], axis=1), jnp.concatenate([cross.T, second], axis=1)], axis=0
    )
    same = iota((size, size), 0) == iota((size, size), 1)
    matrix = matrix + jnp.where(same, size - 1.0, 0.0)
    squares = jnp.sum(jnp.sum(matrix * matrix, axis=0, keepdims=True), axis=1, keepdims=True)
    norm_scale = 0.5 * jnp.sqrt(squares)
    inverse_scale = 1.0 / norm_scale
    diagonal = jnp.where(same, 1.5, 0.0)
    first_split = split(matrix)
    second_power = dot3(first_split, first_split, halves=True)
    third_power = dot3(first_split, split(second_power), halves=True)
    product = matrix * inverse_scale
    inverse_iter = diagonal - 0.5 * product
    product = (
        2.25 * product
        - (1.5 * inverse_scale**2) * second_power
        + (0.25 * inverse_scale**3) * third_power
    )
    for newton_step in range(1, NSTEPS):
        factor = split(product)
        if newton_step < NSTEPS - 1:
            square = dot3(factor, factor)
            inverse_step = dot3(split(inverse_iter), factor)
            cube = dot3(factor, split(square), halves=True)
            product = 2.25 * product - 1.5 * square + 0.25 * cube
        else:
            inverse_step = dot3(split(inverse_iter), factor, halves=True)
        inverse_iter = 1.5 * inverse_iter - 0.5 * inverse_step
    root = inverse_iter * (1.0 / jnp.sqrt(norm_scale))
    innovation = jnp.concatenate([extra[0:1], extra[1:2]], axis=1)
    inner = jnp.sum(root * innovation, axis=1, keepdims=True)
    mean_shift = jnp.sum(inner * root, axis=0, keepdims=True)
    transform = (math.sqrt(size - 1.0) * root + mean_shift).astype(BF16)
    copies = []
    for step, at in enumerate(range(0, anomaly_ref.shape[1], WIDTH)):
        span = slice(at, at + WIDTH)
        combined = dot(transform, anomaly_ref[:, span]) + average_ref[:, span]
        block_ref[:, span] = combined.astype(BF16)
        copy = pltpu.make_async_copy(
            block_ref.at[:, span], output_ref.at[:, span], semaphores.at[step]
        )
        copy.start()
        copies.append(copy)
    for copy in copies:
        copy.wait()


def call(
    kernel,
    shapes,
    *args,
    scratch=(),
    limit=VMEM_LIMIT,
    scalars=0,
    space=pltpu.VMEM,
    inputs=pltpu.VMEM,
):
    spaces = [pltpu.SMEM] * scalars + [inputs] * (len(args) - scalars)
    return pl.pallas_call(
        kernel,
        out_shape=shapes,
        in_specs=[pl.BlockSpec(memory_space=where) for where in spaces],
        out_specs=jax.tree.map(lambda _: pl.BlockSpec(memory_space=space), shapes),
        scratch_shapes=scratch,
        compiler_params=pltpu.CompilerParams(vmem_limit_bytes=limit),
    )(*args)


def step(ensemble, obs_anomaly, innovation, obs_precision, owner_region, neighbours):
    regions = lax.axis_size("region")
    levels = lax.axis_size("level")
    my_region = lax.axis_index("region")
    my_level = lax.axis_index("level")
    members = obs_anomaly.shape[2]
    local_obs = obs_anomaly.shape[1]
    capacity = 3 * local_obs // (2 * regions)
    places = regions // GROUPS
    owners = owner_region.reshape(1, local_obs)
    listed = neighbours.T
    shape = jax.ShapeDtypeStruct
    block = (places, GROUPS * capacity, members)
    rows = call(
        functools.partial(place_kernel, regions, capacity),
        shape(block, BF16),
        owners,
        obs_precision,
        obs_anomaly[0],
        limit=FIRST_LIMIT,
        space=pl.ANY,
        inputs=pl.ANY,
        scratch=[
            pltpu.VMEM(owners.shape, jnp.int32),
            pltpu.VMEM(obs_precision.shape, BF16),
            pltpu.VMEM((local_obs, members), BF16),
            pltpu.VMEM(block, BF16),
            pltpu.SemaphoreType.DMA((3,)),
            pltpu.SemaphoreType.DMA((4,)),
        ],
    )
    near = [[region_at(place, group) for place in range(places)] for group in range(GROUPS)]
    routed = lax.all_to_all(rows, "region", 0, 0, tiled=True, axis_index_groups=near)
    piece = members // places
    high, low = call(
        weight_kernel, (shape((regions * SUBLANES, regions * SUBLANES), BF16),) * 2, listed
    )
    sums = call(
        sums_kernel,
        shape((GROUPS, places * ROWS, LANES), BF16),
        owners,
        obs_precision,
        innovation,
        obs_anomaly[0],
        listed,
    )
    my_group = my_region // CORES % PLANES // PAIR

    def group_pairs(ahead):
        pairs = []
        for region in range(regions):
            x, z, core = region_parts(region)
            pairs.append((region, (x * PLANES + (z + PAIR * ahead) % PLANES) * CORES + core))
        return pairs

    total = lax.dynamic_index_in_dim(sums, my_group, 0, keepdims=False).astype(F32)
    for ahead in (1, GROUPS - 1):
        sent = lax.dynamic_index_in_dim(sums, (my_group + ahead) % GROUPS, 0, keepdims=False)
        arrived_part = lax.ppermute(sent, "region", group_pairs(ahead))
        total = total + arrived_part.astype(F32)
    far = lax.dynamic_index_in_dim(sums, (my_group + 2) % GROUPS, 0, keepdims=False)
    total = jnp.concatenate([total.astype(BF16), far], axis=0)
    block = (places, GROUPS * piece + EXTRA, LANES)
    message = call(
        functools.partial(covariance_kernel, capacity),
        shape(block, BF16),
        routed,
        total,
        space=pltpu.HBM,
        scratch=[pltpu.VMEM(block, BF16), pltpu.SemaphoreType.DMA((2,))],
    )
    message = lax.all_to_all(message, "region", 0, 0, tiled=True, axis_index_groups=near)
    mixed, part = call(
        mix_kernel,
        (shape((regions, piece, LANES), BF16), shape((2, members + LANES), F32)),
        message,
        high,
        low,
    )
    pieces = lax.all_to_all(mixed, "region", 0, 0, tiled=True)

    arrived_part = lax.ppermute(part[1:2], "region", group_pairs(2))
    part = part[0:1] + arrived_part
    height = members + SUBLANES
    own, sent = call(
        gather_kernel, (shape((height, LANES), F32), shape((height, LANES), BF16)), pieces, part
    )
    arrived = []
    for ahead in range(1, levels):
        pairs = [(level, (level + ahead) % levels) for level in range(levels)]
        arrived.append(lax.ppermute(sent, "level", pairs))
    columns = ensemble.shape[2]
    average, anomaly = call(
        anomaly_kernel,
        (shape((1, columns), F32), shape((members, columns), BF16)),
        ensemble[0],
        limit=FIRST_LIMIT,
    )
    analysis = call(
        functools.partial(transform_kernel, levels),
        shape((members, columns), BF16),
        my_level.astype(jnp.int32).reshape(1),
        average,
        anomaly,
        own,
        *arrived,
        scalars=1,
        space=pl.ANY,
        scratch=[
            pltpu.VMEM((members, columns), BF16),
            pltpu.SemaphoreType.DMA((columns // WIDTH,)),
        ],
    )
    return analysis[None]


def solution(mesh):
    return jax.shard_map(
        step,
        mesh=mesh,
        in_specs=(
            P("level", None, "region"),
            P("level", "region", None),
            P("level", "region"),
            P("level", "region"),
            P("level", "region", None),
            P(),
        ),
        out_specs=P("level", None, "region"),
        check_vma=False,
    )
```

```python
import functools
import math

import jax
import jax.numpy as jnp
from jax import lax
from jax.experimental import pallas as pl
from jax.experimental.pallas import tpu as pltpu
from jax.sharding import PartitionSpec as P


NSTEPS = 4
TAPER = 0.6
DECAY = 0.5
LANES, SUBLANES = 128, 8
COLUMNS, PLANES, CORES = 4, 8, 2
PAIR = 2
GROUPS = PLANES // PAIR
WIDTH = 512
ROWS = 3
EXTRA = 8
VMEM_LIMIT = 16 << 20
FIRST_LIMIT = 62 << 20
BF16 = jnp.bfloat16
F32 = jnp.float32


def iota(shape, dim):
    return lax.broadcasted_iota(jnp.int32, shape, dim)


def dot(left, right, dims=((1,), (0,))):
    return lax.dot_general(left, right, (dims, ((), ())), preferred_element_type=F32)


def split(value):
    high = value.astype(BF16)
    return high, (value - high.astype(F32)).astype(BF16)


def dot3(left, right, dims=((1,), (0,)), halves=False):
    lh, ll = left
    rh, rl = right
    if dims != ((1,), (0,)):
        return dot(lh, rh, dims) + (dot(lh, rl, dims) + dot(ll, rh, dims))
    left = jnp.concatenate([lh, lh, ll], axis=1)
    right = jnp.concatenate([rh, rl, rh], axis=0)
    half = left.shape[0] // 2
    if halves and half >= LANES:
        return jnp.concatenate([dot(left[:half], right), dot(left[half:], right)], axis=0)
    return dot(left, right)


def region_parts(region):
    return region // (PLANES * CORES), region // CORES % PLANES, region % CORES


def site(region):
    x, z, core = region_parts(region)
    place = (core * PAIR + z % PAIR) * COLUMNS + x
    return place * GROUPS + z // PAIR


def region_at(place, group):
    core, z, x = place // (PAIR * COLUMNS), place // COLUMNS % PAIR, place % COLUMNS
    return (x * PLANES + group * PAIR + z) * CORES + core


def weights_transposed(listed):
    neigh, regions = listed.shape
    owner = iota((regions, regions), 0)
    weight = (owner == iota((regions, regions), 1)).astype(F32)
    for place in range(neigh):
        weight = weight + TAPER ** (place + 1) * (listed[place : place + 1, :] == owner).astype(F32)
    return weight


def onehot(hit):
    return hit.astype(F32).astype(BF16)


def place_kernel(
    regions,
    capacity,
    owner_in,
    precision_in,
    obs_in,
    rows_out,
    owner_ref,
    precision_ref,
    obs_ref,
    rows_ref,
    arrivals,
    departures,
):
    copies = [
        pltpu.make_async_copy(source, target, arrivals.at[index])
        for index, (source, target) in enumerate(
            [(owner_in, owner_ref), (precision_in, precision_ref), (obs_in, obs_ref)]
        )
    ]
    for copy in copies:
        copy.start()
    count = owner_ref.shape[1]
    blocks = count // LANES
    region_ids = iota((regions, LANES), 0)
    earlier = iota((LANES, LANES), 0) < iota((LANES, LANES), 1)
    counter = jnp.concatenate([onehot(earlier), jnp.ones((LANES, LANES), BF16)], axis=1)
    copies[0].wait()
    owners = owner_ref[...]
    named = [region_ids == owners[:, b * LANES : (b + 1) * LANES] for b in range(blocks)]
    ranks = dot(jnp.concatenate([onehot(hit) for hit in named], axis=0), counter)
    base = (site(region_ids) * capacity).astype(F32)
    pieces = []
    for b in range(blocks):
        part = ranks[b * regions : (b + 1) * regions]
        slot = jnp.where(named[b], part[:, :LANES] + base, 0.0)
        pieces.append(jnp.sum(slot, axis=0, keepdims=True))
        base = base + part[:, LANES:]
    slots = jnp.concatenate(pieces, axis=1).astype(jnp.int32)
    copies[1].wait()
    precision = precision_ref[...].astype(F32)
    scale = jnp.sqrt(precision)
    copies[2].wait()
    obs = obs_ref[...]

    span = GROUPS * capacity
    at_once = 4
    leaving = []
    sites = regions // GROUPS
    for start in range(0, sites, at_once):
        hit = slots == iota((at_once * span, count), 0) + start * span
        placed = dot(jnp.where(hit, scale, 0.0).astype(BF16), obs).astype(BF16)
        for k in range(at_once):
            rows_ref[start + k] = placed[k * span : (k + 1) * span]
        part = slice(start, start + at_once)
        copy = pltpu.make_async_copy(
            rows_ref.at[part], rows_out.at[part], departures.at[start // at_once]
        )
        copy.start()
        leaving.append(copy)
    for copy in leaving:
        copy.wait()


def sums_kernel(owner_ref, precision_ref, innovation_ref, obs_ref, listed_ref, sums_ref):
    count = owner_ref.shape[1]
    regions = listed_ref.shape[1]
    groups, lines, _ = sums_ref.shape
    obs = obs_ref[...]
    precision = precision_ref[...].astype(F32)
    factor = precision * innovation_ref[...].astype(F32)
    hit = iota((regions, count), 0) == owner_ref[...]
    sums = dot(jnp.where(hit, factor, 0.0).astype(BF16), obs)
    half = obs[:, LANES:].astype(F32)
    squares = dot(jnp.where(hit, precision, 0.0).astype(BF16), (half * half).astype(BF16))
    weight = split(weights_transposed(listed_ref[...]))
    row = iota((regions, groups * lines), 1)
    region = region_at(row % lines // ROWS, row // lines)
    pick = onehot(iota((regions, groups * lines), 0) == region)
    chosen = split(dot(weight[0], pick) + dot(weight[1], pick))
    over = ((0,), (0,))
    parts = [dot3(chosen, split(value), over) for value in (sums[:, :LANES], sums[:, LANES:], squares)]
    kind = iota((groups * lines, LANES), 0) % ROWS
    mixed = jnp.where(kind == 0, parts[0], jnp.where(kind == 1, parts[1], parts[2]))
    sums_ref[...] = mixed.astype(BF16).reshape(groups, lines, LANES)


def weight_kernel(listed_ref, high_ref, low_ref):
    size = high_ref.shape[0]
    weight = split(weights_transposed(listed_ref[...]))
    regions = listed_ref.shape[1]
    expand = onehot(iota((regions, size), 0) == iota((regions, size), 1) // SUBLANES)
    rows = split(dot(weight[0], expand) + dot(weight[1], expand))
    at = iota((regions, size), 1) // SUBLANES
    spread = onehot(iota((regions, size), 0) == region_at(at // GROUPS, at % GROUPS))
    over = ((0,), (0,))
    full = dot(rows[0], spread, over) + dot(rows[1], spread, over)
    same = iota((size, size), 0) % SUBLANES == iota((size, size), 1) % SUBLANES
    high, low = split(jnp.where(same, full, 0.0))
    high_ref[...] = high
    low_ref[...] = low


def covariance_kernel(capacity, rows_ref, sums_ref, message_out, message_ref, semaphores):
    half = LANES
    members = rows_ref.shape[2]
    places = message_ref.shape[0]
    piece = members // places
    above = iota((half, half), 0) <= iota((half, half), 1)
    for group in range(GROUPS):
        rows = rows_ref[:, group * capacity : (group + 1) * capacity, :].reshape(-1, members)
        total = dot(rows, rows, ((0,), (0,)))
        corner = jnp.where(above, total[:half, :half], total[half:, half:])
        packed = jnp.concatenate([corner, total[:half, half:]], axis=0).astype(BF16)
        message_ref[:, group * piece : (group + 1) * piece, :] = packed.reshape(places, piece, LANES)
        if group == GROUPS // 2 - 1:
            part = slice(0, (group + 1) * piece)
            first = pltpu.make_async_copy(
                message_ref.at[:, part], message_out.at[:, part], semaphores.at[0]
            )
            first.start()
    wide = (places * EXTRA, places * ROWS)
    line = iota(wide, 0)
    spread = (line % EXTRA < ROWS) & (line // EXTRA * ROWS + line % EXTRA == iota(wide, 1))
    sums = dot(onehot(spread), sums_ref[...]).astype(BF16)
    message_ref[:, GROUPS * piece :, :] = sums.reshape(places, EXTRA, LANES)
    part = slice(GROUPS // 2 * piece, GROUPS * piece + EXTRA)
    second = pltpu.make_async_copy(
        message_ref.at[:, part], message_out.at[:, part], semaphores.at[1]
    )
    second.start()
    first.wait()
    second.wait()


def mix_kernel(message_ref, high_ref, low_ref, mixed_ref, sums_ref):
    regions, piece, _ = mixed_ref.shape
    span = GROUPS * piece
    message = message_ref[:, :span, :].reshape(regions, piece, LANES)
    sums = jnp.sum(message_ref[:, span:, :].astype(F32), axis=0)
    sums_ref[...] = jnp.concatenate([sums[part : part + 1] for part in range(3)], axis=1)
    parts = [
        message[:, at : at + SUBLANES, :].reshape(regions * SUBLANES, LANES) for at in range(0, piece, SUBLANES)
    ]
    wide = jnp.concatenate(parts, axis=1)
    mixed = (dot(high_ref[...], wide) + dot(low_ref[...], wide)).astype(BF16)
    for part in range(len(parts)):
        at = part * SUBLANES
        block = mixed[:, part * LANES : (part + 1) * LANES]
        mixed_ref[:, at : at + SUBLANES, :] = block.reshape(regions, SUBLANES, LANES)


def gather_kernel(pieces_ref, extra_ref, own_ref, sent_ref):
    regions, piece, _ = pieces_ref.shape
    size = regions // GROUPS * piece
    for place in range(regions // GROUPS):
        total = pieces_ref[region_at(place, 0)].astype(F32)
        for group in range(1, GROUPS):
            total = total + pieces_ref[region_at(place, group)].astype(F32)
        own_ref[place * piece : (place + 1) * piece, :] = total
        sent_ref[place * piece : (place + 1) * piece, :] = total.astype(BF16)
    extra = extra_ref[...]
    high = extra.astype(BF16).astype(F32)
    low = extra - high
    rows = [value[:, at : at + LANES] for value in (high, low) for at in range(0, 3 * LANES, LANES)]
    rows = jnp.concatenate(rows + [jnp.zeros((2, LANES), F32)], axis=0)
    own_ref[size:, :] = rows
    sent_ref[size:, :] = rows.astype(BF16)


def anomaly_kernel(ensemble_ref, average_ref, anomaly_ref):
    members, columns = ensemble_ref.shape
    for at in range(0, columns, WIDTH):
        block = ensemble_ref[:, at : at + WIDTH].astype(F32)
        average = jnp.sum(block, axis=0, keepdims=True) * (1.0 / members)
        average_ref[:, at : at + WIDTH] = average
        anomaly_ref[:, at : at + WIDTH] = (block - average).astype(BF16)


def transform_kernel(levels, level_ref, average_ref, anomaly_ref, own_ref, *refs):
    half = LANES
    size = 2 * half
    output_ref, block_ref, semaphores = refs[-3:]
    level = level_ref[0]
    everything = own_ref[...]
    for ahead in range(1, levels):
        source = lax.rem(level + (levels - ahead), levels)
        apart = jnp.abs(level - source)
        factor = jnp.where(apart == 1, DECAY, jnp.where(apart == 2, DECAY**2, DECAY**3))
        everything = everything + factor * refs[ahead - 1][...].astype(F32)
    extra = everything[size : size + 3] + everything[size + 3 : size + 6]
    tri = everything[:half]
    tri_t = tri.T
    cross = everything[half:size]
    row = iota((half, half), 0)
    col = iota((half, half), 1)
    first = jnp.where(row <= col, tri, tri_t)
    second = jnp.where(row > col, tri, tri_t)
    second = jnp.where(row == col, extra[2:3], second)
    matrix = jnp.concatenate(
        [jnp.concatenate([first, cross], axis=1), jnp.concatenate([cross.T, second], axis=1)], axis=0
    )
    same = iota((size, size), 0) == iota((size, size), 1)
    matrix = matrix + jnp.where(same, size - 1.0, 0.0)
    squares = jnp.sum(jnp.sum(matrix * matrix, axis=0, keepdims=True), axis=1, keepdims=True)
    norm_scale = 0.5 * jnp.sqrt(squares)
    inverse_scale = 1.0 / norm_scale
    diagonal = jnp.where(same, 1.5, 0.0)
    first_split = split(matrix)
    second_power = dot3(first_split, first_split, halves=True)
    third_power = dot3(first_split, split(second_power), halves=True)
    product = matrix * inverse_scale
    inverse_iter = diagonal - 0.5 * product
    product = (
        2.25 * product
        - (1.5 * inverse_scale**2) * second_power
        + (0.25 * inverse_scale**3) * third_power
    )
    for newton_step in range(1, NSTEPS):
        factor = split(product)
        if newton_step < NSTEPS - 1:
            square = dot3(factor, factor)
            inverse_step = dot3(split(inverse_iter), factor)
            cube = dot3(factor, split(square), halves=True)
            product = 2.25 * product - 1.5 * square + 0.25 * cube
        else:
            inverse_step = dot3(split(inverse_iter), factor, halves=True)
        inverse_iter = 1.5 * inverse_iter - 0.5 * inverse_step
    root = inverse_iter * (1.0 / jnp.sqrt(norm_scale))
    innovation = jnp.concatenate([extra[0:1], extra[1:2]], axis=1)
    inner = jnp.sum(root * innovation, axis=1, keepdims=True)
    mean_shift = jnp.sum(inner * root, axis=0, keepdims=True)
    transform = (math.sqrt(size - 1.0) * root + mean_shift).astype(BF16)
    copies = []
    for step, at in enumerate(range(0, anomaly_ref.shape[1], WIDTH)):
        span = slice(at, at + WIDTH)
        combined = dot(transform, anomaly_ref[:, span]) + average_ref[:, span]
        block_ref[:, span] = combined.astype(BF16)
        copy = pltpu.make_async_copy(
            block_ref.at[:, span], output_ref.at[:, span], semaphores.at[step]
        )
        copy.start()
        copies.append(copy)
    for copy in copies:
        copy.wait()


def call(
    kernel,
    shapes,
    *args,
    scratch=(),
    limit=VMEM_LIMIT,
    scalars=0,
    space=pltpu.VMEM,
    inputs=pltpu.VMEM,
):
    spaces = [pltpu.SMEM] * scalars + [inputs] * (len(args) - scalars)
    return pl.pallas_call(
        kernel,
        out_shape=shapes,
        in_specs=[pl.BlockSpec(memory_space=where) for where in spaces],
        out_specs=jax.tree.map(lambda _: pl.BlockSpec(memory_space=space), shapes),
        scratch_shapes=scratch,
        compiler_params=pltpu.CompilerParams(vmem_limit_bytes=limit),
    )(*args)


def step(ensemble, obs_anomaly, innovation, obs_precision, owner_region, neighbours):
    regions = lax.axis_size("region")
    levels = lax.axis_size("level")
    my_region = lax.axis_index("region")
    my_level = lax.axis_index("level")
    members = obs_anomaly.shape[2]
    local_obs = obs_anomaly.shape[1]
    capacity = 3 * local_obs // (2 * regions)
    places = regions // GROUPS
    owners = owner_region.reshape(1, local_obs)
    listed = neighbours.T
    shape = jax.ShapeDtypeStruct
    block = (places, GROUPS * capacity, members)
    rows = call(
        functools.partial(place_kernel, regions, capacity),
        shape(block, BF16),
        owners,
        obs_precision,
        obs_anomaly[0],
        limit=FIRST_LIMIT,
        space=pl.ANY,
        inputs=pl.ANY,
        scratch=[
            pltpu.VMEM(owners.shape, jnp.int32),
            pltpu.VMEM(obs_precision.shape, BF16),
            pltpu.VMEM((local_obs, members), BF16),
            pltpu.VMEM(block, BF16),
            pltpu.SemaphoreType.DMA((3,)),
            pltpu.SemaphoreType.DMA((4,)),
        ],
    )
    near = [[region_at(place, group) for place in range(places)] for group in range(GROUPS)]
    routed = lax.all_to_all(rows, "region", 0, 0, tiled=True, axis_index_groups=near)
    piece = members // places
    high, low = call(
        weight_kernel, (shape((regions * SUBLANES, regions * SUBLANES), BF16),) * 2, listed
    )
    sums = call(
        sums_kernel,
        shape((GROUPS, places * ROWS, LANES), BF16),
        owners,
        obs_precision,
        innovation,
        obs_anomaly[0],
        listed,
    )
    my_group = my_region // CORES % PLANES // PAIR
    total = lax.dynamic_index_in_dim(sums, my_group, 0, keepdims=False).astype(F32)
    for ahead in range(1, GROUPS):
        sent = lax.dynamic_index_in_dim(sums, (my_group + ahead) % GROUPS, 0, keepdims=False)
        pairs = []
        for region in range(regions):
            x, z, core = region_parts(region)
            pairs.append((region, (x * PLANES + (z + PAIR * ahead) % PLANES) * CORES + core))
        arrived_part = lax.ppermute(sent, "region", pairs)
        total = total + arrived_part.astype(F32)
    total = total.astype(BF16)
    block = (places, GROUPS * piece + EXTRA, LANES)
    message = call(
        functools.partial(covariance_kernel, capacity),
        shape(block, BF16),
        routed,
        total,
        space=pltpu.HBM,
        scratch=[pltpu.VMEM(block, BF16), pltpu.SemaphoreType.DMA((2,))],
    )
    message = lax.all_to_all(message, "region", 0, 0, tiled=True, axis_index_groups=near)
    mixed, part = call(
        mix_kernel,
        (shape((regions, piece, LANES), BF16), shape((1, members + LANES), F32)),
        message,
        high,
        low,
    )
    pieces = lax.all_to_all(mixed, "region", 0, 0, tiled=True)

    height = members + SUBLANES
    own, sent = call(
        gather_kernel, (shape((height, LANES), F32), shape((height, LANES), BF16)), pieces, part
    )
    arrived = []
    for ahead in range(1, levels):
        pairs = [(level, (level + ahead) % levels) for level in range(levels)]
        arrived.append(lax.ppermute(sent, "level", pairs))
    columns = ensemble.shape[2]
    average, anomaly = call(
        anomaly_kernel,
        (shape((1, columns), F32), shape((members, columns), BF16)),
        ensemble[0],
        limit=FIRST_LIMIT,
    )
    analysis = call(
        functools.partial(transform_kernel, levels),
        shape((members, columns), BF16),
        my_level.astype(jnp.int32).reshape(1),
        average,
        anomaly,
        own,
        *arrived,
        scalars=1,
        space=pl.ANY,
        scratch=[
            pltpu.VMEM((members, columns), BF16),
            pltpu.SemaphoreType.DMA((columns // WIDTH,)),
        ],
    )
    return analysis[None]


def solution(mesh):
    return jax.shard_map(
        step,
        mesh=mesh,
        in_specs=(
            P("level", None, "region"),
            P("level", "region", None),
            P("level", "region"),
            P("level", "region"),
            P("level", "region", None),
            P(),
        ),
        out_specs=P("level", None, "region"),
        check_vma=False,
    )
```
